32 devices in a mesh: groups: 2 (over x), patch: 16 (over z, y, core).
Axes of the slice: x: 2, y: 2, z: 4, core: 2. Of those that a mesh axis runs over, the one named last changes fastest.
Arguments:
- node_latents: bfloat16 [16384, 512], P(('groups', 'patch')), parts along dimension 0, may hold values from -6 to 6
- edge_latents: bfloat16 [32768, 512], P(('groups', 'patch')), parts along dimension 0, may hold values from -6 to 6
- fine_senders: int32 [16, 768], P('patch'), may hold values from 0 to 639
- coarse_owners: int32 [16, 256, 1], P('patch'), may hold values from 0 to 15; in each aligned block of 256 rows (0 to 255, 256 to 511, ..., all dimensions but the last counted through in order) at most 32 rows name the same one
- coarse_slots: int32 [16, 256], P('patch'), may hold values from 0 to 19
- coarse_nodes: int32 [16, 20], P('patch'), may hold values from 0 to 511
- receivers: int32 [16, 1024], P('patch'), may hold values from 0 to 511, never falling along the last dimension, each value on 1 to 4 neighbouring positions
- block_fill: int32 [16, 8], P('patch'), may hold values from 64 to 128
- node_cotangent: bfloat16 [16384, 512], P(('groups', 'patch')), parts along dimension 0, may hold values from -6 to 6
- edge_cotangent: bfloat16 [32768, 512], P(('groups', 'patch')), parts along dimension 0, may hold values from -6 to 6
- edge_first: bfloat16 [1536, 512], replicated, may hold values from -0.15625 to 0.15625
- edge_bias: float32 [512], replicated, may hold values from -3 to 3
- edge_second: bfloat16 [512, 512], replicated, may hold values from -0.25 to 0.25
- edge_shift: float32 [512], replicated, may hold values from -3 to 3
- edge_gain: float32 [512], replicated, may hold values from 0.5 to 1.5
- node_first: bfloat16 [1024, 512], replicated, may hold values from -0.1875 to 0.1875
- node_bias: float32 [512], replicated, may hold values from -3 to 3
- node_second: bfloat16 [512, 512], replicated, may hold values from -0.25 to 0.25
- node_shift: float32 [512], replicated, may hold values from -3 to 3
- node_gain: float32 [512], replicated, may hold values from 0.5 to 1.5
Outputs:
- new_nodes: bfloat16 [16384, 512], P(('groups', 'patch')), parts along dimension 0
- new_edges: bfloat16 [32768, 512], P(('groups', 'patch')), parts along dimension 0
- node_grads: bfloat16 [16384, 512], P(('groups', 'patch')), parts along dimension 0
- edge_grads: bfloat16 [32768, 512], P(('groups', 'patch')), parts along dimension 0
The draws below stay inside these ranges and needn't reach their ends.
There are 2 independent parts, one for each index of `groups`. The reference program is written for one: setup_inputs(seed, part) draws one part's arguments, and reference() takes and returns one part's arrays. A program takes and returns all parts, laid end to end along the dimension named above; an argument that names none is the same for every part. Nothing has to cross between parts.
Inputs may be any that keep to these rules, and one draw needn't show every extreme that they name: `fine_senders`: index i < 64 is row 448 + i of the patch before; 64 <= i < 576 is own row i - 64; beyond, row i - 576 of the patch after. `coarse_owners`: among the coarse edge slots of one patch at most 32 name the same owner, and some patch reaches 32. `receivers`: never falling along the edge slots of one patch; every node receives some slot. The first block_fill slots of a block are live edges, the rest padding.
All inputs are finite; a program needn't handle non-finite values.
Results may differ from the reference program's by a relative error of at most 0.0055.
Values may be sent and summed in bfloat16 or wider, within the bound.
A program may use at most 128 MiB of HBM per device.

```python
import math
import jax
import jax.numpy as jnp
import numpy as np
from jax import lax

D = 512
NODE_DEV = 512
HALO = 64
COARSE_DEV = 20
BLK = 128
BLOCKS_DEV = 8
FINE_DEV = 768
CE_DEV = 256
EDGES_DEV = 1024
CAP = 32
NODES = 8192
EDGES = 16384
N_PATCH = 16


def touch_ends(drawn, own_key, low, high):
    dims = drawn.shape
    spot = [jax.random.randint(jax.random.fold_in(own_key, axis), (), 0, dims[axis]) for axis in range(len(dims))]
    drawn = drawn.at[tuple(spot)].set(low)
    longest = dims.index(max(dims))
    spot[longest] = (spot[longest] + 1) % dims[longest]
    return drawn.at[tuple(spot)].set(high)


def shard_levels(rng, extent, cuts, least, top_value):
    def one(dim, parts):
        draws = jax.random.uniform(jax.random.fold_in(jax.random.fold_in(rng, 6), dim), (parts,), jnp.float32, least / len(cuts), top_value / len(cuts))
        return jnp.repeat(jnp.exp(draws), extent[dim] // parts).reshape((-1,) + (1,) * (len(extent) - dim - 1))

    loudness = one(*cuts[0])
    for cut in cuts[1:]:
        loudness = loudness * one(*cut)
    return loudness


def split_up(amount, total, most, skew):
    loads = [(1 << 20) // math.isqrt(grade ** skew) + 1 for grade in range(2, amount + 1)]
    surplus, counts = total - most - (amount - 1), [1] * (amount - 1)
    while surplus > 0:
        movable = [i for i in range(amount - 1) if counts[i] < most]
        mass, budget = sum([loads[i] for i in movable]), surplus
        for i in movable:
            extra = min(most - counts[i], max(1, budget * loads[i] // mass), surplus)
            counts[i] = counts[i] + extra
            surplus = surplus - extra
    return np.array([most] + counts)


def uneven_parts(key, count, total, bound, slope):
    if count == 2:
        one = jax.random.randint(key, (), max(1, total - bound), min(bound, total - 1) + 1)
        return jnp.stack([one, total - one])
    tallies = jnp.asarray(split_up(count, total, bound, slope), jnp.int32)
    couples = (count - 1) // 2
    source_of, receiver = tallies[1:1 + 2 * couples:2], tallies[2:2 + 2 * couples:2]
    room = jnp.minimum(source_of - 1, bound - receiver)
    passed = jax.random.randint(jax.random.fold_in(key, 1), (couples,), 0, 1 << 20) % (room + 1)
    tallies = tallies.at[1:1 + 2 * couples:2].set(source_of - passed).at[2:2 + 2 * couples:2].set(receiver + passed)
    return tallies[jax.random.permutation(jax.random.fold_in(key, 2), count)]


def assign_block(stream_key, own, number, rows, number_of, top, limit, skew):
    order = jax.random.permutation(stream_key, number_of)
    heavy_load, ordinary = portions_of(number_of, rows * top, limit, skew, True), portions_of(number_of, rows * top, limit, skew, False)
    places = jnp.arange(number_of)

    def named(sizes, offset_by):
        used = int((sizes > 0).sum())
        fixed = max(1, used // 4)
        passed = fixed + (places - fixed + offset_by * (used - fixed)) % max(1, number_of - fixed)
        return jnp.zeros((number_of,), jnp.int32).at[order[jnp.where(places < fixed, places, passed)]].set(jnp.asarray(sizes, jnp.int32))

    sizes = jnp.where(number % 4 == 0, named(heavy_load, number // 4), named(ordinary, number - number // 4 - 1))
    mixed = jax.random.permutation(jax.random.fold_in(own, 3), number_of)
    giver, receiver = mixed[0:number_of // 2 * 2:2], mixed[1:number_of // 2 * 2:2]
    room = jnp.minimum(sizes[giver] - 1, limit - sizes[receiver]) // 2
    room = jnp.where((giver == order[0]) | (receiver == order[0]) | (sizes[receiver] == 0), 0, jnp.maximum(room, 0))
    passed = jax.random.randint(jax.random.fold_in(own, 4), (number_of // 2,), 0, 1 << 20) % (room + 1)
    sizes = sizes.at[giver].add(-passed).at[receiver].add(passed)
    items = jnp.searchsorted(jnp.cumsum(sizes), jnp.arange(rows * top), side="right").astype(jnp.int32)
    grid = items.reshape(top, rows).T
    grid = grid[jax.random.permutation(jax.random.fold_in(own, 1), rows)]
    offset_by = jax.random.randint(jax.random.fold_in(own, 2), (rows, 1), 0, top)
    return jnp.take_along_axis(grid, (jnp.arange(top)[None, :] + offset_by) % top, axis=1)


def portions_of(amount, total, most, skew, full):
    portions = [(1 << 20) // math.isqrt(rank ** skew) + 1 for rank in range(1, amount + 1)]
    largest = most if full else min(most, max(-(-total // amount), total * portions[0] // sum(portions)))
    least = 1 if total - largest >= amount - 1 else 0
    holding, rest = [largest] + [least] * (amount - 1), total - largest - least * (amount - 1)
    while rest > 0:
        candidates = [i for i in range(1, amount) if holding[i] < largest] or [i for i in range(1, amount) if holding[i] < most]
        whole, left = sum([portions[i] for i in candidates]), rest
        for i in candidates:
            more = min(most - holding[i], max(1, left * portions[i] // whole), rest)
            holding[i] = holding[i] + more
            rest = rest - more
    return np.array(holding)


def gaussian(own_key, shape, deviation, most, pieces=(), kind=jnp.bfloat16):
    values = deviation * jax.random.normal(own_key, shape, jnp.float32)
    if pieces:
        values = values * shard_levels(own_key, shape, pieces, -0.22, 0.18)
    return jnp.clip(values, -most, most).astype(kind)


def setup_inputs(seed: int = 0, part: int = 0) -> dict:
    key_list = jax.random.split(jax.random.key(seed), 21)
    own_keys = jax.random.split(jax.random.fold_in(key_list[20], part), 21)
    node_latents = gaussian(own_keys[0], (NODES, D), 1.0, 6.0, ((0, 16),))
    edge_latents = gaussian(own_keys[1], (EDGES, D), 1.0, 6.0, ((0, 16),))
    fine_senders = touch_ends(jax.random.randint(key_list[2], (N_PATCH, FINE_DEV), 0, NODE_DEV + 2 * HALO), jax.random.fold_in(key_list[2], 1), 0, (NODE_DEV + 2 * HALO) - 1).astype(jnp.int32)
    coarse_owners_keys = jax.random.split(jax.random.fold_in(key_list[3], 1), N_PATCH * CE_DEV // CE_DEV)
    coarse_owners_turns = jax.random.permutation(jax.random.fold_in(key_list[3], 3), N_PATCH * CE_DEV // CE_DEV)
    coarse_owners = jax.vmap(lambda own, number: assign_block(jax.random.fold_in(key_list[3], 2), own, number, CE_DEV, N_PATCH, 1, CAP, 2))(coarse_owners_keys, coarse_owners_turns).reshape((N_PATCH, CE_DEV, 1))
    coarse_slots = touch_ends(jax.random.randint(key_list[4], (N_PATCH, CE_DEV), 0, COARSE_DEV), jax.random.fold_in(key_list[4], 1), 0, COARSE_DEV - 1).astype(jnp.int32)
    coarse_nodes = touch_ends(jax.random.randint(key_list[5], (N_PATCH, COARSE_DEV), 0, NODE_DEV), jax.random.fold_in(key_list[5], 1), 0, NODE_DEV - 1).astype(jnp.int32)
    receivers = jax.vmap(lambda own: jnp.searchsorted(jnp.cumsum(uneven_parts(own, NODE_DEV, EDGES_DEV, max(2, 2 * EDGES_DEV // NODE_DEV), 2)), jnp.arange(EDGES_DEV), side="right"))(jax.random.split(key_list[6], N_PATCH)).reshape((N_PATCH, EDGES_DEV)).astype(jnp.int32)
    block_fill = touch_ends(jax.random.randint(key_list[7], (N_PATCH, BLOCKS_DEV), BLK // 2, BLK + 1), jax.random.fold_in(key_list[7], 1), BLK // 2, BLK).astype(jnp.int32)
    node_cotangent = gaussian(own_keys[8], (NODES, D), 1.0, 6.0, ((0, 16),))
    edge_cotangent = gaussian(own_keys[9], (EDGES, D), 1.0, 6.0, ((0, 16),))
    edge_first = gaussian(key_list[10], (3 * D, D), (3 * D) ** -0.5, 0.15625)
    edge_bias = gaussian(key_list[11], (D,), 0.5, 3.0, (), jnp.float32)
    edge_second = gaussian(key_list[12], (D, D), D ** -0.5, 0.25)
    edge_shift = gaussian(key_list[13], (D,), 0.5, 3.0, (), jnp.float32)
    edge_gain = jnp.clip(1.0 + 0.1 * jax.random.normal(key_list[14], (D,), jnp.float32), 0.5, 1.5)
    node_first = gaussian(key_list[15], (2 * D, D), (2 * D) ** -0.5, 0.1875)
    node_bias = gaussian(key_list[16], (D,), 0.5, 3.0, (), jnp.float32)
    node_second = gaussian(key_list[17], (D, D), D ** -0.5, 0.25)
    node_shift = gaussian(key_list[18], (D,), 0.5, 3.0, (), jnp.float32)
    node_gain = jnp.clip(1.0 + 0.1 * jax.random.normal(key_list[19], (D,), jnp.float32), 0.5, 1.5)
    return dict(node_latents=node_latents, edge_latents=edge_latents, fine_senders=fine_senders, coarse_owners=coarse_owners, coarse_slots=coarse_slots, coarse_nodes=coarse_nodes, receivers=receivers, block_fill=block_fill, node_cotangent=node_cotangent, edge_cotangent=edge_cotangent, edge_first=edge_first, edge_bias=edge_bias, edge_second=edge_second, edge_shift=edge_shift, edge_gain=edge_gain, node_first=node_first, node_bias=node_bias, node_second=node_second, node_shift=node_shift, node_gain=node_gain)


def layer_norm(values):
    centered = values - lax.optimization_barrier(jnp.mean(values, axis=-1, keepdims=True))
    inverse = lax.rsqrt(lax.optimization_barrier(jnp.mean(centered * centered, axis=-1, keepdims=True)) + 1e-05)
    return (centered * inverse, inverse)

def norm_back(upstream, normed, inverse):
    return inverse * (upstream - lax.optimization_barrier(jnp.mean(upstream, axis=-1, keepdims=True)) - normed * lax.optimization_barrier(jnp.mean(upstream * normed, axis=-1, keepdims=True)))

def forward_product(inputs, weight):
    return jnp.dot(inputs, weight, preferred_element_type=jnp.float32)

def backward_product(gradient, weight):
    return lax.dot_general(gradient, weight, (((1,), (1,)), ((), ())), preferred_element_type=jnp.float32)

def silu_slope(values):
    sigmoid_value = jax.nn.sigmoid(values)
    return sigmoid_value * (1.0 + values * (1.0 - sigmoid_value))

def local_pass(edge_rows, node_rows, senders, receivers, block_fill, edge_cotangent, node_cotangent, edge_first, edge_bias, edge_second, edge_shift, edge_gain, node_first, node_bias, node_second, node_shift, node_gain):
    feature_width = node_rows.shape[1]
    node_count = node_rows.shape[0]
    block_len = edge_rows.shape[0] // block_fill.shape[0]
    live_mask = (jnp.arange(block_len, dtype=jnp.int32)[None, :] < block_fill[:, None]).reshape(-1)
    live_mask = live_mask.astype(jnp.float32)[:, None]
    receiving = node_rows[receivers]
    w_edge = edge_first[:feature_width]
    w_send = edge_first[feature_width:2 * feature_width]
    w_recv = edge_first[2 * feature_width:]
    pre_edge = forward_product(edge_rows, w_edge) + forward_product(senders, w_send) + forward_product(receiving, w_recv) + edge_bias
    hidden = jax.nn.silu(pre_edge).astype(jnp.bfloat16)
    normed, inverse = layer_norm(forward_product(hidden, edge_second) + edge_shift)
    update = normed * edge_gain * live_mask
    new_edges = (edge_rows + update).astype(jnp.bfloat16)
    summed = jax.ops.segment_sum(update, receivers, num_segments=node_count)
    w_node = node_first[:feature_width]
    w_summed = node_first[feature_width:]
    pre_node = forward_product(node_rows, w_node) + forward_product(summed.astype(jnp.bfloat16), w_summed) + node_bias
    node_hidden = jax.nn.silu(pre_node).astype(jnp.bfloat16)
    node_normed, node_inverse = layer_norm(forward_product(node_hidden, node_second) + node_shift)
    new_nodes = (node_rows + node_normed * node_gain).astype(jnp.bfloat16)
    node_upstream = node_cotangent.astype(jnp.float32)
    node_back = norm_back(node_upstream * node_gain, node_normed, node_inverse).astype(jnp.bfloat16)
    node_pre_grad = (backward_product(node_back, node_second) * silu_slope(pre_node)).astype(jnp.bfloat16)
    node_grads = node_upstream + backward_product(node_pre_grad, w_node)
    summed_grad = backward_product(node_pre_grad, w_summed)
    edge_upstream = edge_cotangent.astype(jnp.float32)
    update_grad = edge_upstream + summed_grad[receivers]
    edge_back = norm_back(update_grad * edge_gain * live_mask, normed, inverse).astype(jnp.bfloat16)
    pre_grad = (backward_product(edge_back, edge_second) * silu_slope(pre_edge)).astype(jnp.bfloat16)
    edge_grads = (edge_upstream + backward_product(pre_grad, w_edge)).astype(jnp.bfloat16)
    node_grads = node_grads + jax.ops.segment_sum(backward_product(pre_grad, w_recv), receivers, num_segments=node_count)
    sender_grads = backward_product(pre_grad, w_send)
    return (new_edges, new_nodes, edge_grads, node_grads, sender_grads)

def reference(node_latents, edge_latents, fine_senders, coarse_owners, coarse_slots, coarse_nodes, receivers, block_fill, node_cotangent, edge_cotangent, edge_first, edge_bias, edge_second, edge_shift, edge_gain, node_first, node_bias, node_second, node_shift, node_gain):
    patches = N_PATCH
    feature_width = node_latents.shape[1]
    blocks = node_latents.reshape(patches, NODE_DEV, feature_width)
    rim_left = jnp.roll(blocks[:, NODE_DEV - HALO:], 1, axis=0)
    rim_right = jnp.roll(blocks[:, :HALO], -1, axis=0)
    extended = jnp.concatenate([rim_left, blocks, rim_right], axis=1)
    coarse_table = jax.vmap(lambda rows_here, chosen: rows_here[chosen])(blocks, coarse_nodes)
    coarse_table = coarse_table.reshape(patches * COARSE_DEV, feature_width)
    table_index = (coarse_owners[:, :, 0] * COARSE_DEV + coarse_slots).astype(jnp.int32)

    def per_patch(patch_items):
        edge_rows, node_rows, extended_rows, fine_index, coarse_index, receiving, fill_here, edge_grad_in, node_grad_in = patch_items
        senders = jnp.concatenate([extended_rows[fine_index], coarse_table[coarse_index]], axis=0)
        result = local_pass(edge_rows, node_rows, senders, receiving, fill_here, edge_grad_in, node_grad_in, edge_first, edge_bias, edge_second, edge_shift, edge_gain, node_first, node_bias, node_second, node_shift, node_gain)
        halo_grads = jax.ops.segment_sum(result[4][:FINE_DEV], fine_index, num_segments=NODE_DEV + 2 * HALO)
        return (result[0], result[1], result[2], result[3], halo_grads, result[4][FINE_DEV:])
    outputs = lax.map(per_patch, (edge_latents.reshape(patches, EDGES_DEV, feature_width), blocks, extended, fine_senders, table_index, receivers, block_fill, edge_cotangent.reshape(patches, EDGES_DEV, feature_width), node_cotangent.reshape(patches, NODE_DEV, feature_width)))
    new_edges, new_nodes, edge_grads, node_grads, halo_grads, coarse_grads = outputs
    node_grads = node_grads + halo_grads[:, HALO:HALO + NODE_DEV]
    node_grads = node_grads.at[:, NODE_DEV - HALO:].add(jnp.roll(halo_grads[:, :HALO], -1, axis=0))
    node_grads = node_grads.at[:, :HALO].add(jnp.roll(halo_grads[:, HALO + NODE_DEV:], 1, axis=0))
    table_grads = jax.ops.segment_sum(coarse_grads.reshape(-1, feature_width), table_index.reshape(-1), num_segments=patches * COARSE_DEV)
    table_grads = table_grads.reshape(patches, COARSE_DEV, feature_width)
    node_grads = node_grads + jax.vmap(lambda grads_here, chosen: jax.ops.segment_sum(grads_here, chosen, num_segments=NODE_DEV))(table_grads, coarse_nodes)
    return (new_nodes.reshape(-1, feature_width), new_edges.reshape(-1, feature_width), node_grads.astype(jnp.bfloat16).reshape(-1, feature_width), edge_grads.reshape(-1, feature_width))
```

```python
import functools

import jax
import jax.numpy as jnp
from jax import lax
from jax.experimental import pallas as pl
from jax.experimental.pallas import tpu as pltpu
from jax.sharding import PartitionSpec as P

HALO = 64
REACH = 4
ROWS = 256
TILE = 16
LANES = 128
MESH = pl.DeviceIdType.MESH
F32 = jnp.float32
BF16 = jnp.bfloat16
LIMIT = 59000 * 1024
LAST = 8 * 1024 * 1024


def mm(a, b):
    return jnp.dot(a, b, preferred_element_type=F32)


def mm_t(a, b):
    return lax.dot_general(a, b, (((1,), (1,)), ((), ())), preferred_element_type=F32)


def onehot(mask):
    return jnp.where(mask, 1.0, 0.0).astype(BF16)


def pick_rows(index_row, width, base=0):
    parts = []
    for k in range(index_row.shape[1] // LANES):
        chunk = jnp.broadcast_to(index_row[:, k * LANES : (k + 1) * LANES], (LANES, LANES))
        column = jnp.transpose(chunk)
        lane = lax.broadcasted_iota(jnp.int32, (LANES, LANES), 1)
        parts.append(
            jnp.concatenate(
                [onehot(column == lane + (base + j * LANES)) for j in range(width // LANES)], axis=1
            )
        )
    return jnp.concatenate(parts, axis=0)


def put_rows(index_row, low, count):
    rows = lax.broadcasted_iota(jnp.int32, (count, index_row.shape[1]), 0) + low
    return onehot(rows == index_row)


def sigmoid(values):
    return 0.5 * jnp.tanh(0.5 * values) + 0.5


def norm(values):
    centered = values - jnp.mean(values, axis=-1, keepdims=True)
    inverse = lax.rsqrt(jnp.mean(centered * centered, axis=-1, keepdims=True) + 1e-05)
    return centered * inverse, inverse


def norm_back(upstream, normed, inverse):
    return inverse * (
        upstream
        - jnp.mean(upstream, axis=-1, keepdims=True)
        - normed * jnp.mean(upstream * normed, axis=-1, keepdims=True)
    )


def edge_band(first, edges, count):
    last = first + ROWS - 1
    low = max(first // REACH, first - (edges - count))
    high = min(last, count - 1 - (edges - 1 - last) // REACH)
    return low // LANES * LANES, -(-(high + 1) // LANES) * LANES


def node_band(first, edges, count):
    last = first + ROWS - 1
    low = max(first, edges - REACH * (count - first))
    high = min(REACH * last + REACH - 1, last + edges - count)
    return low // LANES * LANES, -(-(high + 1) // LANES) * LANES


def greet(n):
    me = lax.axis_index("patch")
    barrier = pltpu.get_barrier_semaphore()
    chips = n // 2
    core = lax.rem(me, 2)
    chip = me // 2
    peers = [lax.rem(chip + k, chips) * 2 + core for k in range(1, chips)]
    peers += [chip * 2 + 1 - core, lax.rem(me + 1, n), lax.rem(me + n - 1, n)]
    for peer in peers:
        pl.semaphore_signal(barrier, inc=1, device_id={"patch": peer}, device_id_type=MESH)
    return barrier, len(peers)


def remote(src, dst, send, recv, peer):
    return pltpu.make_async_remote_copy(
        src_ref=src, dst_ref=dst, send_sem=send, recv_sem=recv,
        device_id={"patch": peer}, device_id_type=MESH,
    )


def rows_of(start, size):
    return pl.ds(pl.multiple_of(start, TILE), size)


def order_of(owner, n):
    return lax.rem(owner, 2) * (n // 2) + owner // 2


def bits_order(owner, n):
    return (owner & 1) * (n // 2) + (owner >> 1)


def kernel_layer(
    n, tail, block,
    node_hbm, cnodes_hbm, first_hbm, edge_hbm, receivers_hbm, senders_hbm, bias_hbm,
    second_hbm, shift_hbm, gain_hbm, fill_hbm, owners_hbm, slots_hbm,
    nfirst_hbm, nbias_hbm, nsecond_hbm, nshift_hbm, ngain_hbm, ncot_hbm, ecot_hbm,
    out_node, out_edge, out_egrad, grads, rim_in, served, w_send,
    node, cnodes, w_edge, w_recv, edge, receivers, senders, bias,
    second, shift, gain, fill, owners, slots,
    nfirst, nbias, nsecond, nshift, ngain, ncot, ecot,
    halo, part_recv, part_send, part_halo,
    pre, normed, inverse, update, gagg, gpre, gnpre,
    rows, tabs, leaving, staying, theirs, joined, rim,
    load, halo_send, halo_recv, chip_send, chip_recv, core_send, core_recv,
    rim_send, rim_recv, back_send, back_recv, swap_send, swap_recv,
):
    me = lax.axis_index("patch")
    chips = n // 2
    core = lax.rem(me, 2)
    chip = me // 2
    partner = chip * 2 + 1 - core
    edges, width = edge.shape
    count = node.shape[0]
    fine = senders.shape[1]
    chunks = width // LANES
    half = chips * TILE

    pairs = [
        (node_hbm, node), (cnodes_hbm, cnodes),
        (first_hbm.at[pl.ds(2 * width, width)], w_recv), (first_hbm.at[pl.ds(width, width)], w_send),
        (bias_hbm, bias), (receivers_hbm, receivers), (senders_hbm, senders),
        (first_hbm.at[pl.ds(0, width)], w_edge), (edge_hbm, edge),
        (second_hbm, second), (shift_hbm, shift), (gain_hbm, gain), (fill_hbm, fill),
        (owners_hbm, owners), (slots_hbm, slots),
        (nfirst_hbm, nfirst), (nbias_hbm, nbias), (nsecond_hbm, nsecond), (nshift_hbm, nshift),
        (ngain_hbm, ngain), (ncot_hbm, ncot), (ecot_hbm, ecot),
    ]
    loads = [
        pltpu.make_async_copy(source, target, load.at[i])
        for i, (source, target) in enumerate(pairs)
    ]
    waited = []

    def need(count_of):
        while len(waited) < count_of:
            loads[len(waited)].wait()
            waited.append(True)

    for copy in loads[:9]:
        copy.start()
    barrier, greeted = greet(n)

    need(2)
    line = lax.broadcasted_iota(jnp.int32, (2 * TILE, LANES), 0)
    wanted = jnp.full((2 * TILE, LANES), -1, jnp.int32)
    for k in range(TILE + tail):
        wanted = jnp.where(line == k, cnodes[0, k], wanted)
    lane = lax.broadcasted_iota(jnp.int32, (2 * TILE, LANES), 1)
    chosen = jnp.concatenate(
        [onehot(wanted == lane + k * LANES) for k in range(count // LANES)], axis=1
    )
    own = order_of(me, n)
    mine = rows_of(own * TILE, TILE)
    table = mm(chosen, node[...])
    rows[...] = jnp.zeros_like(rows)
    for c in range(chunks):
        rows[c * tail : (c + 1) * tail, :] = table[TILE : TILE + tail, c * LANES : (c + 1) * LANES]
    tabs[mine, 0:width] = table[0:TILE, :].astype(BF16)
    tabs[mine, width : width + LANES] = rows[...].astype(BF16)

    pl.semaphore_wait(barrier, greeted)
    spread = []
    for k in range(1, chips):
        copy = remote(
            tabs.at[mine], tabs.at[mine], chip_send.at[k], chip_recv.at[k],
            lax.rem(chip + k, chips) * 2 + core,
        )
        copy.start()
        spread.append(copy)
    across = [remote(tabs.at[mine], tabs.at[mine], core_send.at[0], core_recv.at[0], partner)]
    across[0].start()
    up = remote(
        node.at[pl.ds(count - HALO, HALO)], halo.at[pl.ds(0, HALO)],
        halo_send.at[0], halo_recv.at[0], lax.rem(me + 1, n),
    )
    down = remote(
        node.at[pl.ds(0, HALO)], halo.at[pl.ds(HALO, HALO)],
        halo_send.at[1], halo_recv.at[1], lax.rem(me + n - 1, n),
    )
    up.start()
    down.start()
    for copy in loads[9:]:
        copy.start()

    def advance(b):
        part = pl.ds(b * ROWS, ROWS)
        half_pre = 0.5 * pre[part, :]
        bent = jnp.tanh(half_pre)
        more = 1.0 + bent
        active = half_pre * more
        pre[part, :] = more + active * (1.0 - bent)
        result = mm(active.astype(BF16), second[...]) + shift[...]
        centered = result - jnp.mean(result, axis=-1, keepdims=True)
        scale = lax.rsqrt(jnp.mean(centered * centered, axis=-1, keepdims=True) + 1e-05)
        live = []
        for k in range(ROWS // block):
            row = lax.broadcasted_iota(jnp.int32, (block, 1), 0)
            live.append(jnp.where(row < fill[0, b * (ROWS // block) + k], 1.0, 0.0))
        scale = scale * jnp.concatenate(live, axis=0)
        unit = centered * scale
        normed[part, :] = unit
        inverse[part, :] = jnp.broadcast_to(0.5 * scale, (ROWS, LANES))
        change = unit * gain[...]
        update[part, :] = change.astype(BF16)
        out_edge[part, :] = (edge[part, :].astype(F32) + change).astype(BF16)

    need(7)
    part_recv[...] = (mm(node[...], w_recv[...]) + bias[...]).astype(BF16)
    part_send[...] = mm(node[...], w_send[...]).astype(BF16)
    need(9)
    index = senders[...]
    inner = index - HALO
    outer = jnp.where(index < HALO, index, jnp.where(index >= HALO + count, index - count, -1))
    for b in range(edges // ROWS):
        part = pl.ds(b * ROWS, ROWS)
        low, high = edge_band(b * ROWS, edges, count)
        left = [edge[part, :], pick_rows(receivers[:, b * ROWS : (b + 1) * ROWS], high - low, low)]
        right = [w_edge[...], part_recv[low:high, :]]
        if b < fine // ROWS:
            left.append(pick_rows(inner[:, b * ROWS : (b + 1) * ROWS], count))
            right.append(part_send[...])
        pre[part, :] = mm(jnp.concatenate(left, axis=1), jnp.concatenate(right, axis=0))
    up.wait()
    down.wait()
    part_halo[...] = mm(halo[...], w_send[...]).astype(BF16)
    for b in range(fine // ROWS):
        part = pl.ds(b * ROWS, ROWS)
        picked = pick_rows(outer[:, b * ROWS : (b + 1) * ROWS], 2 * HALO)
        pre[part, :] += mm(picked, part_halo[...])
    need(15)
    for b in range(fine // ROWS):
        advance(b)

    for k in range(1, chips):
        source = core * chips + lax.rem(chip + chips - k, chips)
        there = tabs.at[rows_of(source * TILE, TILE)]
        remote(there, there, chip_send.at[k], chip_recv.at[k], partner).wait_recv()
        copy = remote(there, there, core_send.at[k], core_recv.at[k], partner)
        copy.start()
        across.append(copy)

    def turn(b):
        part = pl.ds(b * ROWS, ROWS)
        here = node[part, :]
        low, high = node_band(b * ROWS, edges, count)
        summed = mm(put_rows(receivers[:, low:high], b * ROWS, ROWS), update[low:high, :])
        values = mm(jnp.concatenate([here, summed.astype(BF16)], axis=1), nfirst[...]) + nbias[...]
        half_values = 0.5 * values
        bent = jnp.tanh(half_values)
        more = 1.0 + bent
        active = half_values * more
        slope = more + active * (1.0 - bent)
        result, scale = norm(mm(active.astype(BF16), nsecond[...]) + nshift[...])
        out_node[part, :] = (here.astype(F32) + result * ngain[...]).astype(BF16)
        back = norm_back(ncot[part, :].astype(F32) * ngain[...], result, 0.5 * scale)
        inner_grad = (mm_t(back.astype(BF16), nsecond[...]) * slope).astype(BF16)
        gnpre[part, :] = inner_grad
        gagg[part, :] = mm_t(inner_grad, nfirst[width:, :]).astype(BF16)

    def retreat(b):
        part = pl.ds(b * ROWS, ROWS)
        low, high = edge_band(b * ROWS, edges, count)
        picked = pick_rows(receivers[:, b * ROWS : (b + 1) * ROWS], high - low, low)
        upstream = (ecot[part, :].astype(F32) + mm(picked, gagg[low:high, :])) * gain[...]
        back = norm_back(upstream, normed[part, :], inverse[part, 0:1])
        gpre[part, :] = (mm_t(back.astype(BF16), second[...]) * pre[part, :]).astype(BF16)

    need(21)
    turn(0)

    for copy in across:
        copy.wait()
    for copy in spread:
        copy.wait_send()
    place = bits_order(owners[...], n) * TILE
    slot = slots[...]
    main_key = jnp.where(slot < TILE, place + slot, -1)
    tail_keys = [
        jnp.where(slot >= TILE, place + (slot - TILE) + c * tail, -1) for c in range(chunks)
    ]
    gathered = mm(pick_rows(main_key, n * TILE), tabs[:, 0:width])
    tails = [mm(pick_rows(key, n * TILE), tabs[:, width : width + LANES]) for key in tail_keys]
    sent = (gathered + jnp.concatenate(tails, axis=1)).astype(BF16)
    coarse = pl.ds(fine, edges - fine)
    pre[coarse, :] += mm(sent, w_send[...])
    for b in range(fine // ROWS, edges // ROWS):
        advance(b)
    for b in range(1, count // ROWS):
        turn(b)

    need(22)
    for b in range(fine // ROWS, edges // ROWS):
        retreat(b)

    def returned(base, target):
        target[:, 0:width] = mm(put_rows(main_key, base, half), gpre[coarse, :]).astype(BF16)
        packed = jnp.zeros((half, LANES), F32)
        for c in range(chunks):
            packed = packed + mm(
                put_rows(tail_keys[c], base, half), gpre[coarse, c * LANES : (c + 1) * LANES]
            )
        target[:, width:] = packed.astype(BF16)

    returned((1 - core) * half, leaving)
    swap = remote(leaving, theirs, swap_send.at[0], swap_recv.at[0], partner)
    swap.start()
    returned(core * half, staying)
    retreat(0)
    swap.wait()
    joined[...] = (staying[...].astype(F32) + theirs[...].astype(F32)).astype(BF16)
    served[0:TILE, :] = joined[rows_of(chip * TILE, TILE), :]
    spread = []
    for k in range(1, chips):
        target = lax.rem(chip + k, chips)
        copy = remote(
            joined.at[rows_of(target * TILE, TILE)], served.at[pl.ds(k * TILE, TILE)],
            back_send.at[k], back_recv.at[k], target * 2 + core,
        )
        copy.start()
        spread.append(copy)
    for b in range(1, fine // ROWS):
        retreat(b)

    rim[...] = mm(put_rows(outer, 0, 2 * HALO), gpre[0:fine, :]).astype(BF16)
    down = remote(
        rim.at[pl.ds(0, HALO)], rim_in.at[pl.ds(0, HALO)],
        rim_send.at[0], rim_recv.at[0], lax.rem(me + n - 1, n),
    )
    up = remote(
        rim.at[pl.ds(HALO, HALO)], rim_in.at[pl.ds(HALO, HALO)],
        rim_send.at[1], rim_recv.at[1], lax.rem(me + 1, n),
    )
    down.start()
    up.start()

    for b in range(edges // ROWS):
        part = pl.ds(b * ROWS, ROWS)
        out_egrad[part, :] = (
            ecot[part, :].astype(F32) + mm_t(gpre[part, :], w_edge[...])
        ).astype(BF16)
    for b in range(count // ROWS):
        part = pl.ds(b * ROWS, ROWS)
        by_sender = mm(put_rows(inner, b * ROWS, ROWS), gpre[0:fine, :]).astype(BF16)
        low, high = node_band(b * ROWS, edges, count)
        table = put_rows(receivers[:, low:high], b * ROWS, ROWS)
        by_receiver = mm(table, gpre[low:high, :]).astype(BF16)
        grads[part, :] = ncot[part, :].astype(F32) + mm_t(
            jnp.concatenate([gnpre[part, :], by_receiver, by_sender], axis=1),
            jnp.concatenate([nfirst[0:width, :], w_recv[...], w_send[...]], axis=1),
        )
    down.wait()
    up.wait()
    for copy in spread:
        copy.wait()


def kernel_finish(
    tail, cnodes, out_node, out_edge, out_egrad, grads, rim_in, served, w_send,
    new_nodes, new_edges, node_grads, edge_grads,
    out_ngrad, rows, store,
):
    count, width = grads.shape
    chunks = width // LANES
    puts = [
        pltpu.make_async_copy(source, target, store.at[i])
        for i, (source, target) in enumerate(
            ((out_edge, new_edges), (out_egrad, edge_grads), (out_node, new_nodes))
        )
    ]
    for put in puts:
        put.start()
    sums = served[0:TILE, :].astype(F32)
    for k in range(1, served.shape[0] // TILE):
        sums = sums + served[k * TILE : (k + 1) * TILE, :].astype(F32)
    rows[0:TILE, :] = sums[:, 0:width]
    rows[TILE:, :] = jnp.zeros((rows.shape[0] - TILE, width), F32)
    for c in range(chunks):
        rows[TILE : TILE + tail, c * LANES : (c + 1) * LANES] = sums[
            c * tail : (c + 1) * tail, width:
        ]
    arrived = jnp.concatenate([rim_in[...], rows[...].astype(BF16)], axis=0)
    changes = mm_t(arrived, w_send[...])
    coarse = changes[2 * HALO :, :].astype(BF16)
    lane = lax.broadcasted_iota(jnp.int32, (1, rows.shape[0]), 1)
    wanted = jnp.full((1, rows.shape[0]), -1, jnp.int32)
    for k in range(TILE + tail):
        wanted = jnp.where(lane == k, cnodes[0, k], wanted)
    for b in range(count // ROWS):
        part = pl.ds(b * ROWS, ROWS)
        added = grads[part, :] + mm(put_rows(wanted, b * ROWS, ROWS), coarse)
        low, high = b * ROWS, (b + 1) * ROWS
        pieces = []
        if low == 0:
            pieces.append((added[0:HALO, :] + changes[HALO : 2 * HALO, :]).astype(BF16))
        start = HALO if low == 0 else 0
        stop = ROWS - HALO if high == count else ROWS
        pieces.append(added[start:stop, :].astype(BF16))
        if high == count:
            pieces.append((added[stop:, :] + changes[0:HALO, :]).astype(BF16))
        out_ngrad[part, :] = jnp.concatenate(pieces, axis=0)
        put = pltpu.make_async_copy(out_ngrad.at[part], node_grads.at[part], store.at[len(puts)])
        put.start()
        puts.append(put)
    for put in puts:
        put.wait()


VM = pl.BlockSpec(memory_space=pltpu.VMEM)
SM = pl.BlockSpec(memory_space=pltpu.SMEM)
ANY = pl.BlockSpec(memory_space=pl.ANY)


def dma(*shape):
    return pltpu.SemaphoreType.DMA(shape)


def shards(
    node_latents, edge_latents, fine_senders, coarse_owners, coarse_slots, coarse_nodes,
    receivers, block_fill, node_cotangent, edge_cotangent, edge_first, edge_bias, edge_second,
    edge_shift, edge_gain, node_first, node_bias, node_second, node_shift, node_gain,
):
    n = lax.axis_size("patch")
    chips = n // 2
    count, width = node_latents.shape
    edges = edge_latents.shape[0]
    fine = fine_senders.shape[1]
    tail = coarse_nodes.shape[1] - TILE
    owners = coarse_owners.reshape(1, -1)
    wide = width + LANES
    ints = jnp.int32

    def vec(value):
        return value.reshape(1, -1)

    def vm(rows, columns=width, kind=BF16):
        return pltpu.VMEM((rows, columns), kind)

    def like(value, memory=pltpu.VMEM):
        return memory(value.shape, value.dtype)

    *mids, = pl.pallas_call(
        functools.partial(kernel_layer, n, tail, edges // block_fill.shape[1]),
        out_shape=[
            vm(count), vm(edges), vm(edges), vm(count, width, F32), vm(2 * HALO),
            vm(chips * TILE, wide), vm(width),
        ],
        in_specs=[ANY] * 20,
        out_specs=[VM] * 7,
        scratch_shapes=[
            vm(count), like(coarse_nodes, pltpu.SMEM), vm(width), vm(width), vm(edges),
            vm(1, edges, ints), vm(1, fine, ints), vm(1, width, F32),
            vm(width), vm(1, width, F32), vm(1, width, F32), like(block_fill, pltpu.SMEM),
            like(owners), like(coarse_slots),
            vm(2 * width), vm(1, width, F32), vm(width), vm(1, width, F32), vm(1, width, F32),
            vm(count), vm(edges),
            vm(2 * HALO), vm(count), vm(count), vm(2 * HALO),
            vm(edges, width, F32), vm(edges, width, F32), vm(edges, LANES, F32), vm(edges),
            vm(count), vm(edges), vm(count),
            vm(TILE, LANES, F32), vm(n * TILE, wide),
            vm(chips * TILE, wide), vm(chips * TILE, wide), vm(chips * TILE, wide),
            vm(chips * TILE, wide), vm(2 * HALO),
            dma(22), dma(2), dma(2), dma(chips), dma(chips), dma(chips), dma(chips),
            dma(2), dma(2), dma(chips), dma(chips), dma(1), dma(1),
        ],
        compiler_params=pltpu.CompilerParams(
            collective_id=0, has_side_effects=True, vmem_limit_bytes=LIMIT
        ),
        name="layer",
    )(
        node_latents, coarse_nodes, edge_first, edge_latents, receivers, fine_senders,
        vec(edge_bias), edge_second, vec(edge_shift), vec(edge_gain), block_fill, owners,
        coarse_slots, node_first, vec(node_bias), node_second, vec(node_shift),
        vec(node_gain), node_cotangent, edge_cotangent,
    )
    return pl.pallas_call(
        functools.partial(kernel_finish, tail),
        out_shape=[
            jax.ShapeDtypeStruct((count, width), BF16),
            jax.ShapeDtypeStruct((edges, width), BF16),
            jax.ShapeDtypeStruct((count, width), BF16),
            jax.ShapeDtypeStruct((edges, width), BF16),
        ],
        in_specs=[SM] + [VM] * 7,
        out_specs=[ANY] * 4,
        scratch_shapes=[vm(count), vm(2 * TILE, width, F32), dma(3 + count // ROWS)],
        compiler_params=pltpu.CompilerParams(vmem_limit_bytes=LAST),
        name="finish",
    )(coarse_nodes, *mids)


def solution(mesh):
    rows = P(("groups", "patch"), None)
    flat = P("patch", None)
    return jax.shard_map(
        shards,
        mesh=mesh,
        in_specs=(rows, rows, flat, P("patch", None, None), flat, flat, flat, flat, rows, rows)
        + (P(),) * 10,
        out_specs=(rows, rows, rows, rows),
        check_vma=False,
    )
```

```python
import functools

import jax
import jax.numpy as jnp
from jax import lax
from jax.experimental import pallas as pl
from jax.experimental.pallas import tpu as pltpu
from jax.sharding import PartitionSpec as P

HALO = 64
REACH = 4
ROWS = 256
TILE = 16
LANES = 128
MESH = pl.DeviceIdType.MESH
F32 = jnp.float32
BF16 = jnp.bfloat16
LIMIT = 59000 * 1024
LAST = 8 * 1024 * 1024


def mm(a, b):
    return jnp.dot(a, b, preferred_element_type=F32)


def mm_t(a, b):
    return lax.dot_general(a, b, (((1,), (1,)), ((), ())), preferred_element_type=F32)


def onehot(mask):
    return jnp.where(mask, 1.0, 0.0).astype(BF16)


def pick_rows(index_row, width, base=0):
    parts = []
    for k in range(index_row.shape[1] // LANES):
        chunk = jnp.broadcast_to(index_row[:, k * LANES : (k + 1) * LANES], (LANES, LANES))
        column = jnp.transpose(chunk)
        lane = lax.broadcasted_iota(jnp.int32, (LANES, LANES), 1)
        parts.append(
            jnp.concatenate(
                [onehot(column == lane + (base + j * LANES)) for j in range(width // LANES)], axis=1
            )
        )
    return jnp.concatenate(parts, axis=0)


def put_rows(index_row, low, count):
    rows = lax.broadcasted_iota(jnp.int32, (count, index_row.shape[1]), 0) + low
    return onehot(rows == index_row)


def sigmoid(values):
    return 0.5 * jnp.tanh(0.5 * values) + 0.5


def norm(values):
    centered = values - jnp.mean(values, axis=-1, keepdims=True)
    inverse = lax.rsqrt(jnp.mean(centered * centered, axis=-1, keepdims=True) + 1e-05)
    return centered * inverse, inverse


def norm_back(upstream, normed, inverse):
    return inverse * (
        upstream
        - jnp.mean(upstream, axis=-1, keepdims=True)
        - normed * jnp.mean(upstream * normed, axis=-1, keepdims=True)
    )


def edge_band(first, edges, count):
    last = first + ROWS - 1
    low = max(first // REACH, first - (edges - count))
    high = min(last, count - 1 - (edges - 1 - last) // REACH)
    return low // LANES * LANES, -(-(high + 1) // LANES) * LANES


def node_band(first, edges, count):
    last = first + ROWS - 1
    low = max(first, edges - REACH * (count - first))
    high = min(REACH * last + REACH - 1, last + edges - count)
    return low // LANES * LANES, -(-(high + 1) // LANES) * LANES


def greet(n):
    me = lax.axis_index("patch")
    barrier = pltpu.get_barrier_semaphore()
    chips = n // 2
    core = lax.rem(me, 2)
    chip = me // 2
    peers = [lax.rem(chip + k, chips) * 2 + core for k in range(1, chips)]
    peers += [chip * 2 + 1 - core, lax.rem(me + 1, n), lax.rem(me + n - 1, n)]
    for peer in peers:
        pl.semaphore_signal(barrier, inc=1, device_id={"patch": peer}, device_id_type=MESH)
    return barrier, len(peers)


def remote(src, dst, send, recv, peer):
    return pltpu.make_async_remote_copy(
        src_ref=src, dst_ref=dst, send_sem=send, recv_sem=recv,
        device_id={"patch": peer}, device_id_type=MESH,
    )


def rows_of(start, size):
    return pl.ds(pl.multiple_of(start, TILE), size)


def order_of(owner, n):
    return lax.rem(owner, 2) * (n // 2) + owner // 2


def bits_order(owner, n):
    return (owner & 1) * (n // 2) + (owner >> 1)


def kernel_layer(
    n, tail, block,
    node_hbm, cnodes_hbm, first_hbm, edge_hbm, receivers_hbm, senders_hbm, bias_hbm,
    second_hbm, shift_hbm, gain_hbm, fill_hbm, owners_hbm, slots_hbm,
    nfirst_hbm, nbias_hbm, nsecond_hbm, nshift_hbm, ngain_hbm, ncot_hbm, ecot_hbm,
    out_node, out_edge, out_egrad, grads, rim_in, served, w_send,
    node, cnodes, w_edge, w_recv, edge, receivers, senders, bias,
    second, shift, gain, fill, owners, slots,
    nfirst, nbias, nsecond, nshift, ngain, ncot, ecot,
    halo, part_recv, part_send, part_halo,
    pre, normed, inverse, update, gagg, gpre, gnpre,
    rows, tabs, leaving, staying, theirs, joined, rim,
    load, halo_send, halo_recv, chip_send, chip_recv, core_send, core_recv,
    rim_send, rim_recv, back_send, back_recv, swap_send, swap_recv,
):
    me = lax.axis_index("patch")
    chips = n // 2
    core = lax.rem(me, 2)
    chip = me // 2
    partner = chip * 2 + 1 - core
    edges, width = edge.shape
    count = node.shape[0]
    fine = senders.shape[1]
    chunks = width // LANES
    half = chips * TILE

    pairs = [
        (node_hbm, node), (cnodes_hbm, cnodes),
        (first_hbm.at[pl.ds(2 * width, width)], w_recv), (first_hbm.at[pl.ds(width, width)], w_send),
        (bias_hbm, bias), (receivers_hbm, receivers), (senders_hbm, senders),
        (first_hbm.at[pl.ds(0, width)], w_edge), (edge_hbm, edge),
        (second_hbm, second), (shift_hbm, shift), (gain_hbm, gain), (fill_hbm, fill),
        (owners_hbm, owners), (slots_hbm, slots),
        (nfirst_hbm, nfirst), (nbias_hbm, nbias), (nsecond_hbm, nsecond), (nshift_hbm, nshift),
        (ngain_hbm, ngain), (ncot_hbm, ncot), (ecot_hbm, ecot),
    ]
    loads = [
        pltpu.make_async_copy(source, target, load.at[i])
        for i, (source, target) in enumerate(pairs)
    ]
    waited = []

    def need(count_of):
        while len(waited) < count_of:
            loads[len(waited)].wait()
            waited.append(True)

    barrier, greeted = greet(n)
    for copy in loads[:9]:
        copy.start()

    need(1)
    up = remote(
        node.at[pl.ds(count - HALO, HALO)], halo.at[pl.ds(0, HALO)],
        halo_send.at[0], halo_recv.at[0], lax.rem(me + 1, n),
    )
    down = remote(
        node.at[pl.ds(0, HALO)], halo.at[pl.ds(HALO, HALO)],
        halo_send.at[1], halo_recv.at[1], lax.rem(me + n - 1, n),
    )
    need(2)
    line = lax.broadcasted_iota(jnp.int32, (2 * TILE, LANES), 0)
    wanted = jnp.full((2 * TILE, LANES), -1, jnp.int32)
    for k in range(TILE + tail):
        wanted = jnp.where(line == k, cnodes[0, k], wanted)
    lane = lax.broadcasted_iota(jnp.int32, (2 * TILE, LANES), 1)
    chosen = jnp.concatenate(
        [onehot(wanted == lane + k * LANES) for k in range(count // LANES)], axis=1
    )
    own = order_of(me, n)
    mine = rows_of(own * TILE, TILE)
    table = mm(chosen, node[...])
    rows[...] = jnp.zeros_like(rows)
    for c in range(chunks):
        rows[c * tail : (c + 1) * tail, :] = table[TILE : TILE + tail, c * LANES : (c + 1) * LANES]
    tabs[mine, 0:width] = table[0:TILE, :].astype(BF16)
    tabs[mine, width : width + LANES] = rows[...].astype(BF16)

    pl.semaphore_wait(barrier, greeted)
    up.start()
    down.start()
    spread = []
    for k in range(1, chips):
        copy = remote(
            tabs.at[mine], tabs.at[mine], chip_send.at[k], chip_recv.at[k],
            lax.rem(chip + k, chips) * 2 + core,
        )
        copy.start()
        spread.append(copy)
    across = [remote(tabs.at[mine], tabs.at[mine], core_send.at[0], core_recv.at[0], partner)]
    across[0].start()
    for copy in loads[9:]:
        copy.start()

    def advance(b):
        part = pl.ds(b * ROWS, ROWS)
        half_pre = 0.5 * pre[part, :]
        bent = jnp.tanh(half_pre)
        more = 1.0 + bent
        active = half_pre * more
        pre[part, :] = more + active * (1.0 - bent)
        result = mm(active.astype(BF16), second[...]) + shift[...]
        centered = result - jnp.mean(result, axis=-1, keepdims=True)
        scale = lax.rsqrt(jnp.mean(centered * centered, axis=-1, keepdims=True) + 1e-05)
        live = []
        for k in range(ROWS // block):
            row = lax.broadcasted_iota(jnp.int32, (block, 1), 0)
            live.append(jnp.where(row < fill[0, b * (ROWS // block) + k], 1.0, 0.0))
        scale = scale * jnp.concatenate(live, axis=0)
        unit = centered * scale
        normed[part, :] = unit
        inverse[part, :] = jnp.broadcast_to(0.5 * scale, (ROWS, LANES))
        change = unit * gain[...]
        update[part, :] = change.astype(BF16)
        out_edge[part, :] = (edge[part, :].astype(F32) + change).astype(BF16)

    need(7)
    part_recv[...] = (mm(node[...], w_recv[...]) + bias[...]).astype(BF16)
    part_send[...] = mm(node[...], w_send[...]).astype(BF16)
    need(9)
    index = senders[...]
    inner = index - HALO
    outer = jnp.where(index < HALO, index, jnp.where(index >= HALO + count, index - count, -1))

    for b in [*range(fine // ROWS, edges // ROWS), *range(fine // ROWS)]:
        part = pl.ds(b * ROWS, ROWS)
        low, high = edge_band(b * ROWS, edges, count)
        left = [edge[part, :], pick_rows(receivers[:, b * ROWS : (b + 1) * ROWS], high - low, low)]
        right = [w_edge[...], part_recv[low:high, :]]
        if b < fine // ROWS:
            left.append(pick_rows(inner[:, b * ROWS : (b + 1) * ROWS], count))
            right.append(part_send[...])
        pre[part, :] = mm(jnp.concatenate(left, axis=1), jnp.concatenate(right, axis=0))
    need(15)
    up.wait()
    down.wait()
    part_halo[...] = mm(halo[...], w_send[...]).astype(BF16)

    def close_up(b):
        part = pl.ds(b * ROWS, ROWS)
        picked = pick_rows(outer[:, b * ROWS : (b + 1) * ROWS], 2 * HALO)
        pre[part, :] += mm(picked, part_halo[...])
        advance(b)

    close_up(0)
    for k in range(1, chips):
        source = core * chips + lax.rem(chip + chips - k, chips)
        there = tabs.at[rows_of(source * TILE, TILE)]
        remote(there, there, chip_send.at[k], chip_recv.at[k], partner).wait_recv()
        copy = remote(there, there, core_send.at[k], core_recv.at[k], partner)
        copy.start()
        across.append(copy)
    for b in range(1, fine // ROWS):
        close_up(b)

    def turn(b):
        part = pl.ds(b * ROWS, ROWS)
        here = node[part, :]
        low, high = node_band(b * ROWS, edges, count)
        summed = mm(put_rows(receivers[:, low:high], b * ROWS, ROWS), update[low:high, :])
        values = mm(jnp.concatenate([here, summed.astype(BF16)], axis=1), nfirst[...]) + nbias[...]
        half_values = 0.5 * values
        bent = jnp.tanh(half_values)
        more = 1.0 + bent
        active = half_values * more
        slope = more + active * (1.0 - bent)
        result, scale = norm(mm(active.astype(BF16), nsecond[...]) + nshift[...])
        out_node[part, :] = (here.astype(F32) + result * ngain[...]).astype(BF16)
        back = norm_back(ncot[part, :].astype(F32) * ngain[...], result, 0.5 * scale)
        inner_grad = (mm_t(back.astype(BF16), nsecond[...]) * slope).astype(BF16)
        gnpre[part, :] = inner_grad
        gagg[part, :] = mm_t(inner_grad, nfirst[width:, :]).astype(BF16)

    def retreat(b):
        part = pl.ds(b * ROWS, ROWS)
        low, high = edge_band(b * ROWS, edges, count)
        picked = pick_rows(receivers[:, b * ROWS : (b + 1) * ROWS], high - low, low)
        upstream = (ecot[part, :].astype(F32) + mm(picked, gagg[low:high, :])) * gain[...]
        back = norm_back(upstream, normed[part, :], inverse[part, 0:1])
        gpre[part, :] = (mm_t(back.astype(BF16), second[...]) * pre[part, :]).astype(BF16)

    need(22)
    for copy in across:
        copy.wait()
    for copy in spread:
        copy.wait_send()
    place = bits_order(owners[...], n) * TILE
    slot = slots[...]
    main_key = jnp.where(slot < TILE, place + slot, -1)
    tail_keys = [
        jnp.where(slot >= TILE, place + (slot - TILE) + c * tail, -1) for c in range(chunks)
    ]
    gathered = mm(pick_rows(main_key, n * TILE), tabs[:, 0:width])
    tails = [mm(pick_rows(key, n * TILE), tabs[:, width : width + LANES]) for key in tail_keys]
    sent = (gathered + jnp.concatenate(tails, axis=1)).astype(BF16)
    coarse = pl.ds(fine, edges - fine)
    pre[coarse, :] += mm(sent, w_send[...])
    for b in range(fine // ROWS, edges // ROWS):
        advance(b)
    for b in range(count // ROWS):
        turn(b)
    for b in range(fine // ROWS, edges // ROWS):
        retreat(b)

    def returned(base, target):
        target[:, 0:width] = mm(put_rows(main_key, base, half), gpre[coarse, :]).astype(BF16)
        packed = jnp.zeros((half, LANES), F32)
        for c in range(chunks):
            packed = packed + mm(
                put_rows(tail_keys[c], base, half), gpre[coarse, c * LANES : (c + 1) * LANES]
            )
        target[:, width:] = packed.astype(BF16)

    returned((1 - core) * half, leaving)
    swap = remote(leaving, theirs, swap_send.at[0], swap_recv.at[0], partner)
    swap.start()
    returned(core * half, staying)
    retreat(0)
    retreat(1)
    swap.wait()
    joined[...] = (staying[...].astype(F32) + theirs[...].astype(F32)).astype(BF16)
    served[0:TILE, :] = joined[rows_of(chip * TILE, TILE), :]
    spread = []

    def hand(t):
        target = t + jnp.where(chip <= t, 1, 0)
        k = lax.rem(target - chip + chips, chips)
        copy = remote(
            joined.at[rows_of(target * TILE, TILE)], served.at[rows_of(k * TILE, TILE)],
            back_send.at[k], back_recv.at[k], target * 2 + core,
        )
        copy.start()
        spread.append(copy)

    for t in range(1):
        hand(t)
    for b in range(2, fine // ROWS):
        retreat(b)
    rim[...] = mm(put_rows(outer, 0, 2 * HALO), gpre[0:fine, :]).astype(BF16)
    down = remote(
        rim.at[pl.ds(0, HALO)], rim_in.at[pl.ds(0, HALO)],
        rim_send.at[0], rim_recv.at[0], lax.rem(me + n - 1, n),
    )
    up = remote(
        rim.at[pl.ds(HALO, HALO)], rim_in.at[pl.ds(HALO, HALO)],
        rim_send.at[1], rim_recv.at[1], lax.rem(me + 1, n),
    )
    up.start()
    down.start()
    for t in range(1, chips - 1):
        hand(t)

    for b in range(edges // ROWS):
        part = pl.ds(b * ROWS, ROWS)
        out_egrad[part, :] = (
            ecot[part, :].astype(F32) + mm_t(gpre[part, :], w_edge[...])
        ).astype(BF16)
    for b in range(count // ROWS):
        part = pl.ds(b * ROWS, ROWS)
        by_sender = mm(put_rows(inner, b * ROWS, ROWS), gpre[0:fine, :]).astype(BF16)
        low, high = node_band(b * ROWS, edges, count)
        table = put_rows(receivers[:, low:high], b * ROWS, ROWS)
        by_receiver = mm(table, gpre[low:high, :]).astype(BF16)
        grads[part, :] = ncot[part, :].astype(F32) + mm_t(
            jnp.concatenate([gnpre[part, :], by_receiver, by_sender], axis=1),
            jnp.concatenate([nfirst[0:width, :], w_recv[...], w_send[...]], axis=1),
        )
    down.wait()
    up.wait()
    for copy in spread:
        copy.wait()


def kernel_finish(
    tail, cnodes, out_node, out_edge, out_egrad, grads, rim_in, served, w_send,
    new_nodes, new_edges, node_grads, edge_grads,
    out_ngrad, rows, store,
):
    count, width = grads.shape
    chunks = width // LANES
    puts = [
        pltpu.make_async_copy(source, target, store.at[i])
        for i, (source, target) in enumerate(
            ((out_edge, new_edges), (out_egrad, edge_grads), (out_node, new_nodes))
        )
    ]
    for put in puts:
        put.start()
    sums = served[0:TILE, :].astype(F32)
    for k in range(1, served.shape[0] // TILE):
        sums = sums + served[k * TILE : (k + 1) * TILE, :].astype(F32)
    rows[0:TILE, :] = sums[:, 0:width]
    rows[TILE:, :] = jnp.zeros((rows.shape[0] - TILE, width), F32)
    for c in range(chunks):
        rows[TILE : TILE + tail, c * LANES : (c + 1) * LANES] = sums[
            c * tail : (c + 1) * tail, width:
        ]
    arrived = jnp.concatenate([rim_in[...], rows[...].astype(BF16)], axis=0)
    changes = mm_t(arrived, w_send[...])
    coarse = changes[2 * HALO :, :].astype(BF16)
    lane = lax.broadcasted_iota(jnp.int32, (1, rows.shape[0]), 1)
    wanted = jnp.full((1, rows.shape[0]), -1, jnp.int32)
    for k in range(TILE + tail):
        wanted = jnp.where(lane == k, cnodes[0, k], wanted)
    for b in range(count // ROWS):
        part = pl.ds(b * ROWS, ROWS)
        added = grads[part, :] + mm(put_rows(wanted, b * ROWS, ROWS), coarse)
        low, high = b * ROWS, (b + 1) * ROWS
        pieces = []
        if low == 0:
            pieces.append((added[0:HALO, :] + changes[HALO : 2 * HALO, :]).astype(BF16))
        start = HALO if low == 0 else 0
        stop = ROWS - HALO if high == count else ROWS
        pieces.append(added[start:stop, :].astype(BF16))
        if high == count:
            pieces.append((added[stop:, :] + changes[0:HALO, :]).astype(BF16))
        out_ngrad[part, :] = jnp.concatenate(pieces, axis=0)
        put = pltpu.make_async_copy(out_ngrad.at[part], node_grads.at[part], store.at[len(puts)])
        put.start()
        puts.append(put)
    for put in puts:
        put.wait()


VM = pl.BlockSpec(memory_space=pltpu.VMEM)
SM = pl.BlockSpec(memory_space=pltpu.SMEM)
ANY = pl.BlockSpec(memory_space=pl.ANY)


def dma(*shape):
    return pltpu.SemaphoreType.DMA(shape)


def shards(
    node_latents, edge_latents, fine_senders, coarse_owners, coarse_slots, coarse_nodes,
    receivers, block_fill, node_cotangent, edge_cotangent, edge_first, edge_bias, edge_second,
    edge_shift, edge_gain, node_first, node_bias, node_second, node_shift, node_gain,
):
    n = lax.axis_size("patch")
    chips = n // 2
    count, width = node_latents.shape
    edges = edge_latents.shape[0]
    fine = fine_senders.shape[1]
    tail = coarse_nodes.shape[1] - TILE
    owners = coarse_owners.reshape(1, -1)
    wide = width + LANES
    ints = jnp.int32

    def vec(value):
        return value.reshape(1, -1)

    def vm(rows, columns=width, kind=BF16):
        return pltpu.VMEM((rows, columns), kind)

    def like(value, memory=pltpu.VMEM):
        return memory(value.shape, value.dtype)

    *mids, = pl.pallas_call(
        functools.partial(kernel_layer, n, tail, edges // block_fill.shape[1]),
        out_shape=[
            vm(count), vm(edges), vm(edges), vm(count, width, F32), vm(2 * HALO),
            vm(chips * TILE, wide), vm(width),
        ],
        in_specs=[ANY] * 20,
        out_specs=[VM] * 7,
        scratch_shapes=[
            vm(count), like(coarse_nodes, pltpu.SMEM), vm(width), vm(width), vm(edges),
            vm(1, edges, ints), vm(1, fine, ints), vm(1, width, F32),
            vm(width), vm(1, width, F32), vm(1, width, F32), like(block_fill, pltpu.SMEM),
            like(owners), like(coarse_slots),
            vm(2 * width), vm(1, width, F32), vm(width), vm(1, width, F32), vm(1, width, F32),
            vm(count), vm(edges),
            vm(2 * HALO), vm(count), vm(count), vm(2 * HALO),
            vm(edges, width, F32), vm(edges, width, F32), vm(edges, LANES, F32), vm(edges),
            vm(count), vm(edges), vm(count),
            vm(TILE, LANES, F32), vm(n * TILE, wide),
            vm(chips * TILE, wide), vm(chips * TILE, wide), vm(chips * TILE, wide),
            vm(chips * TILE, wide), vm(2 * HALO),
            dma(22), dma(2), dma(2), dma(chips), dma(chips), dma(chips), dma(chips),
            dma(2), dma(2), dma(chips), dma(chips), dma(1), dma(1),
        ],
        compiler_params=pltpu.CompilerParams(
            collective_id=0, has_side_effects=True, vmem_limit_bytes=LIMIT
        ),
        name="layer",
    )(
        node_latents, coarse_nodes, edge_first, edge_latents, receivers, fine_senders,
        vec(edge_bias), edge_second, vec(edge_shift), vec(edge_gain), block_fill, owners,
        coarse_slots, node_first, vec(node_bias), node_second, vec(node_shift),
        vec(node_gain), node_cotangent, edge_cotangent,
    )
    return pl.pallas_call(
        functools.partial(kernel_finish, tail),
        out_shape=[
            jax.ShapeDtypeStruct((count, width), BF16),
            jax.ShapeDtypeStruct((edges, width), BF16),
            jax.ShapeDtypeStruct((count, width), BF16),
            jax.ShapeDtypeStruct((edges, width), BF16),
        ],
        in_specs=[SM] + [VM] * 7,
        out_specs=[ANY] * 4,
        scratch_shapes=[vm(count), vm(2 * TILE, width, F32), dma(3 + count // ROWS)],
        compiler_params=pltpu.CompilerParams(vmem_limit_bytes=LAST),
        name="finish",
    )(coarse_nodes, *mids)


def solution(mesh):
    rows = P(("groups", "patch"), None)
    flat = P("patch", None)
    return jax.shard_map(
        shards,
        mesh=mesh,
        in_specs=(rows, rows, flat, P("patch", None, None), flat, flat, flat, flat, rows, rows)
        + (P(),) * 10,
        out_specs=(rows, rows, rows, rows),
        check_vma=False,
    )
```

```python
import functools

import jax
import jax.numpy as jnp
from jax import lax
from jax.experimental import pallas as pl
from jax.experimental.pallas import tpu as pltpu
from jax.sharding import PartitionSpec as P

HALO = 64
SUB = 32
REACH = 4
ROWS = 256
TILE = 16
LANES = 128
MESH = pl.DeviceIdType.MESH
F32 = jnp.float32
BF16 = jnp.bfloat16
LIMIT = 59000 * 1024
LAST = 8 * 1024 * 1024


def mm(a, b):
    return jnp.dot(a, b, preferred_element_type=F32)


def mm_t(a, b):
    return lax.dot_general(a, b, (((1,), (1,)), ((), ())), preferred_element_type=F32)


def onehot(mask):
    return jnp.where(mask, 1.0, 0.0).astype(BF16)


def pick_rows(index_row, width, base=0):
    parts = []
    for k in range(index_row.shape[1] // LANES):
        chunk = jnp.broadcast_to(index_row[:, k * LANES : (k + 1) * LANES], (LANES, LANES))
        column = jnp.transpose(chunk)
        lane = lax.broadcasted_iota(jnp.int32, (LANES, LANES), 1)
        parts.append(
            jnp.concatenate(
                [onehot(column == lane + (base + j * LANES)) for j in range(width // LANES)], axis=1
            )
        )
    return jnp.concatenate(parts, axis=0)


def put_rows(index_row, low, count):
    rows = lax.broadcasted_iota(jnp.int32, (count, index_row.shape[1]), 0) + low
    return onehot(rows == index_row)


def sigmoid(values):
    return 0.5 * jnp.tanh(0.5 * values) + 0.5


def norm(values):
    centered = values - jnp.mean(values, axis=-1, keepdims=True)
    inverse = lax.rsqrt(jnp.mean(centered * centered, axis=-1, keepdims=True) + 1e-05)
    return centered * inverse, inverse


def norm_back(upstream, normed, inverse):
    return inverse * (
        upstream
        - jnp.mean(upstream, axis=-1, keepdims=True)
        - normed * jnp.mean(upstream * normed, axis=-1, keepdims=True)
    )


def edge_band(first, edges, count):
    last = first + ROWS - 1
    low = max(first // REACH, first - (edges - count))
    high = min(last, count - 1 - (edges - 1 - last) // REACH)
    return low // LANES * LANES, -(-(high + 1) // LANES) * LANES


def node_band(first, edges, count):
    last = first + ROWS - 1
    low = max(first, edges - REACH * (count - first))
    high = min(REACH * last + REACH - 1, last + edges - count)
    return low // LANES * LANES, -(-(high + 1) // LANES) * LANES


def greet(n):
    me = lax.axis_index("patch")
    barrier = pltpu.get_barrier_semaphore()
    chips = n // 2
    core = lax.rem(me, 2)
    chip = me // 2
    peers = [lax.rem(chip + k, chips) * 2 + core for k in range(1, chips)]
    peers += [chip * 2 + 1 - core, lax.rem(me + 1, n), lax.rem(me + n - 1, n)]
    for peer in peers:
        pl.semaphore_signal(barrier, inc=1, device_id={"patch": peer}, device_id_type=MESH)
    return barrier, len(peers)


def remote(src, dst, send, recv, peer):
    return pltpu.make_async_remote_copy(
        src_ref=src, dst_ref=dst, send_sem=send, recv_sem=recv,
        device_id={"patch": peer}, device_id_type=MESH,
    )


def rows_of(start, size):
    return pl.ds(pl.multiple_of(start, TILE), size)


def order_of(owner, n):
    return lax.rem(owner, 2) * (n // 2) + owner // 2


def bits_order(owner, n):
    return (owner & 1) * (n // 2) + (owner >> 1)


def kernel_layer(
    n, tail, block,
    node_hbm, cnodes_hbm, first_hbm, edge_hbm, receivers_hbm, senders_hbm, bias_hbm,
    second_hbm, shift_hbm, gain_hbm, fill_hbm, owners_hbm, slots_hbm,
    nfirst_hbm, nbias_hbm, nsecond_hbm, nshift_hbm, ngain_hbm, ncot_hbm, ecot_hbm,
    out_node, out_edge, out_egrad, grads, rim_in, served, w_send, keys,
    node, cnodes, w_edge, w_recv, edge, receivers, senders, bias,
    second, shift, gain, fill, owners, slots,
    nfirst, nbias, nsecond, nshift, ngain, ncot, ecot,
    halo, part_recv, part_send, part_halo,
    pre, normed, inverse, update, gagg, gpre, gnpre, bent_rows, upper, total,
    rows, tabs, leaving, staying, theirs, joined, rim,
    load, halo_send, halo_recv, chip_send, chip_recv, core_send, core_recv,
    rim_send, rim_recv, back_send, back_recv, swap_send, swap_recv,
):
    me = lax.axis_index("patch")
    chips = n // 2
    core = lax.rem(me, 2)
    chip = me // 2
    partner = chip * 2 + 1 - core
    edges, width = edge.shape
    count = node.shape[0]
    fine = senders.shape[1]
    chunks = width // LANES
    half = chips * TILE
    order = sorted(range(1, chips), key=lambda k: -min(k, chips - k))

    pairs = [
        (node_hbm, node), (cnodes_hbm, cnodes),
        (first_hbm.at[pl.ds(2 * width, width)], w_recv), (first_hbm.at[pl.ds(width, width)], w_send),
        (bias_hbm, bias), (receivers_hbm, receivers), (senders_hbm, senders),
        (first_hbm.at[pl.ds(0, width)], w_edge), (edge_hbm, edge),
        (second_hbm, second), (shift_hbm, shift), (gain_hbm, gain), (fill_hbm, fill),
        (owners_hbm, owners), (slots_hbm, slots),
        (nfirst_hbm, nfirst), (nbias_hbm, nbias), (nsecond_hbm, nsecond), (nshift_hbm, nshift),
        (ngain_hbm, ngain), (ncot_hbm, ncot), (ecot_hbm, ecot),
    ]
    loads = [
        pltpu.make_async_copy(source, target, load.at[i])
        for i, (source, target) in enumerate(pairs)
    ]
    waited = []

    def need(count_of):
        while len(waited) < count_of:
            loads[len(waited)].wait()
            waited.append(True)

    barrier, greeted = greet(n)
    for copy in loads[:9]:
        copy.start()

    need(1)
    up = remote(
        node.at[pl.ds(count - HALO, HALO)], halo.at[pl.ds(0, HALO)],
        halo_send.at[0], halo_recv.at[0], lax.rem(me + 1, n),
    )
    down = remote(
        node.at[pl.ds(0, HALO)], halo.at[pl.ds(HALO, HALO)],
        halo_send.at[1], halo_recv.at[1], lax.rem(me + n - 1, n),
    )
    need(2)
    line = lax.broadcasted_iota(jnp.int32, (2 * TILE, LANES), 0)
    wanted = jnp.full((2 * TILE, LANES), -1, jnp.int32)
    for k in range(TILE + tail):
        wanted = jnp.where(line == k, cnodes[0, k], wanted)
    lane = lax.broadcasted_iota(jnp.int32, (2 * TILE, LANES), 1)
    chosen = jnp.concatenate(
        [onehot(wanted == lane + k * LANES) for k in range(count // LANES)], axis=1
    )
    place_of = lax.broadcasted_iota(jnp.int32, (1, LANES), 1)
    listed = jnp.full((1, LANES), -1, jnp.int32)
    for k in range(TILE + tail):
        listed = jnp.where(place_of == k, cnodes[0, k], listed)
    keys[...] = listed
    own = order_of(me, n)
    mine = rows_of(own * TILE, TILE)
    table = mm(chosen, node[...])
    rows[...] = jnp.zeros_like(rows)
    for c in range(chunks):
        rows[c * tail : (c + 1) * tail, :] = table[TILE : TILE + tail, c * LANES : (c + 1) * LANES]
    tabs[mine, 0:width] = table[0:TILE, :].astype(BF16)
    tabs[mine, width : width + LANES] = rows[...].astype(BF16)

    pl.semaphore_wait(barrier, greeted)
    up.start()
    down.start()
    spread = []
    for k in order:
        copy = remote(
            tabs.at[mine], tabs.at[mine], chip_send.at[k], chip_recv.at[k],
            lax.rem(chip + k, chips) * 2 + core,
        )
        copy.start()
        spread.append(copy)
    across = [remote(tabs.at[mine], tabs.at[mine], core_send.at[0], core_recv.at[0], partner)]
    across[0].start()
    for copy in loads[9:]:
        copy.start()

    def advance(b):
        part = pl.ds(b * ROWS, ROWS)
        for q in range(b * ROWS, (b + 1) * ROWS, SUB):
            few = pl.ds(q, SUB)
            half_pre = 0.5 * pre[few, :]
            bent = jnp.tanh(half_pre)
            more = 1.0 + bent
            active = half_pre * more
            pre[few, :] = more + active * (1.0 - bent)
            bent_rows[few, :] = active.astype(BF16)
        normed[part, :] = mm(bent_rows[part, :], second[...])
        for q in range(b * ROWS, (b + 1) * ROWS, SUB):
            few = pl.ds(q, SUB)
            result = normed[few, :] + shift[...]
            centered = result - jnp.mean(result, axis=-1, keepdims=True)
            scale = lax.rsqrt(jnp.mean(centered * centered, axis=-1, keepdims=True) + 1e-05)
            row = lax.broadcasted_iota(jnp.int32, (SUB, 1), 0) + q % block
            scale = jnp.where(row < fill[0, q // block], scale, 0.0)
            unit = centered * scale
            normed[few, :] = unit
            inverse[few, :] = jnp.broadcast_to(0.5 * scale, (SUB, LANES))
            change = unit * gain[...]
            update[few, :] = change.astype(BF16)
            out_edge[few, :] = (edge[few, :].astype(F32) + change).astype(BF16)

    need(7)
    part_recv[...] = (mm(node[...], w_recv[...]) + bias[...]).astype(BF16)
    part_send[...] = mm(node[...], w_send[...]).astype(BF16)
    need(9)
    index = senders[...]
    inner = index - HALO
    outer = jnp.where(index < HALO, index, jnp.where(index >= HALO + count, index - count, -1))

    for b in [*range(fine // ROWS, edges // ROWS), *range(fine // ROWS)]:
        part = pl.ds(b * ROWS, ROWS)
        low, high = edge_band(b * ROWS, edges, count)
        left = [edge[part, :], pick_rows(receivers[:, b * ROWS : (b + 1) * ROWS], high - low, low)]
        right = [w_edge[...], part_recv[low:high, :]]
        if b < fine // ROWS:
            left.append(pick_rows(inner[:, b * ROWS : (b + 1) * ROWS], count))
            right.append(part_send[...])
        pre[part, :] = mm(jnp.concatenate(left, axis=1), jnp.concatenate(right, axis=0))
    need(15)
    up.wait()
    down.wait()
    part_halo[...] = mm(halo[...], w_send[...]).astype(BF16)

    def close_up(b):
        part = pl.ds(b * ROWS, ROWS)
        picked = pick_rows(outer[:, b * ROWS : (b + 1) * ROWS], 2 * HALO)
        pre[part, :] += mm(picked, part_halo[...])
        advance(b)

    close_up(0)
    for k in order:
        source = core * chips + lax.rem(chip + chips - k, chips)
        there = tabs.at[rows_of(source * TILE, TILE)]
        remote(there, there, chip_send.at[k], chip_recv.at[k], partner).wait_recv()
        copy = remote(there, there, core_send.at[k], core_recv.at[k], partner)
        copy.start()
        across.append(copy)
    for b in range(1, fine // ROWS):
        close_up(b)

    def turn(b):
        part = pl.ds(b * ROWS, ROWS)
        low, high = node_band(b * ROWS, edges, count)
        summed = mm(put_rows(receivers[:, low:high], b * ROWS, ROWS), update[low:high, :])
        total[part, :] = (
            mm(jnp.concatenate([node[part, :], summed.astype(BF16)], axis=1), nfirst[...])
        )
        for q in range(b * ROWS, (b + 1) * ROWS, SUB):
            few = pl.ds(q, SUB)
            half_values = 0.5 * (total[few, :] + nbias[...])
            bent = jnp.tanh(half_values)
            more = 1.0 + bent
            active = half_values * more
            total[few, :] = more + active * (1.0 - bent)
            gnpre[few, :] = active.astype(BF16)
        grads[part, :] = mm(gnpre[part, :], nsecond[...])
        for q in range(b * ROWS, (b + 1) * ROWS, SUB):
            few = pl.ds(q, SUB)
            result, scale = norm(grads[few, :] + nshift[...])
            out_node[few, :] = (node[few, :].astype(F32) + result * ngain[...]).astype(BF16)
            back = norm_back(ncot[few, :].astype(F32) * ngain[...], result, 0.5 * scale)
            gagg[few, :] = back.astype(BF16)
        inner_grad = (mm_t(gagg[part, :], nsecond[...]) * total[part, :]).astype(BF16)
        gnpre[part, :] = inner_grad
        gagg[part, :] = mm_t(inner_grad, nfirst[width:, :]).astype(BF16)

    def retreat(b):
        part = pl.ds(b * ROWS, ROWS)
        low, high = edge_band(b * ROWS, edges, count)
        picked = pick_rows(receivers[:, b * ROWS : (b + 1) * ROWS], high - low, low)
        upper[part, :] = mm(picked, gagg[low:high, :])
        for q in range(b * ROWS, (b + 1) * ROWS, SUB):
            few = pl.ds(q, SUB)
            upstream = (ecot[few, :].astype(F32) + upper[few, :]) * gain[...]
            back = norm_back(upstream, normed[few, :], inverse[few, 0:1])
            bent_rows[few, :] = back.astype(BF16)
        gpre[part, :] = (mm_t(bent_rows[part, :], second[...]) * pre[part, :]).astype(BF16)

    need(22)
    for copy in across:
        copy.wait()
    for copy in spread:
        copy.wait_send()
    place = bits_order(owners[...], n) * TILE
    slot = slots[...]
    main_key = jnp.where(slot < TILE, place + slot, -1)
    tail_keys = [
        jnp.where(slot >= TILE, place + (slot - TILE) + c * tail, -1) for c in range(chunks)
    ]
    gathered = mm(pick_rows(main_key, n * TILE), tabs[:, 0:width])
    tails = [mm(pick_rows(key, n * TILE), tabs[:, width : width + LANES]) for key in tail_keys]
    sent = (gathered + jnp.concatenate(tails, axis=1)).astype(BF16)
    coarse = pl.ds(fine, edges - fine)
    pre[coarse, :] += mm(sent, w_send[...])
    for b in range(fine // ROWS, edges // ROWS):
        advance(b)
    for b in range(count // ROWS):
        turn(b)
    for b in range(fine // ROWS, edges // ROWS):
        retreat(b)

    def returned(base, target):
        target[:, 0:width] = mm(put_rows(main_key, base, half), gpre[coarse, :]).astype(BF16)
        packed = jnp.zeros((half, LANES), F32)
        for c in range(chunks):
            packed = packed + mm(
                put_rows(tail_keys[c], base, half), gpre[coarse, c * LANES : (c + 1) * LANES]
            )
        target[:, width:] = packed.astype(BF16)

    returned((1 - core) * half, leaving)
    swap = remote(leaving, theirs, swap_send.at[0], swap_recv.at[0], partner)
    swap.start()
    returned(core * half, staying)
    for b in range(fine // ROWS):
        retreat(b)
    rim[...] = mm(put_rows(outer, 0, 2 * HALO), gpre[0:fine, :]).astype(BF16)
    down = remote(
        rim.at[pl.ds(0, HALO)], rim_in.at[pl.ds(0, HALO)],
        rim_send.at[0], rim_recv.at[0], lax.rem(me + n - 1, n),
    )
    up = remote(
        rim.at[pl.ds(HALO, HALO)], rim_in.at[pl.ds(HALO, HALO)],
        rim_send.at[1], rim_recv.at[1], lax.rem(me + 1, n),
    )
    up.start()
    down.start()
    swap.wait()
    joined[...] = (staying[...].astype(F32) + theirs[...].astype(F32)).astype(BF16)
    served[0:TILE, :] = joined[rows_of(chip * TILE, TILE), :]
    spread = []

    def hand(t):
        target = t + jnp.where(chip <= t, 1, 0)
        k = lax.rem(target - chip + chips, chips)
        copy = remote(
            joined.at[rows_of(target * TILE, TILE)], served.at[rows_of(k * TILE, TILE)],
            back_send.at[k], back_recv.at[k], target * 2 + core,
        )
        copy.start()
        spread.append(copy)

    for t in range(chips - 1):
        hand(t)

    for b in range(edges // ROWS):
        part = pl.ds(b * ROWS, ROWS)
        out_egrad[part, :] = (
            ecot[part, :].astype(F32) + mm_t(gpre[part, :], w_edge[...])
        ).astype(BF16)
    for b in range(count // ROWS):
        part = pl.ds(b * ROWS, ROWS)
        by_sender = mm(put_rows(inner, b * ROWS, ROWS), gpre[0:fine, :]).astype(BF16)
        low, high = node_band(b * ROWS, edges, count)
        table = put_rows(receivers[:, low:high], b * ROWS, ROWS)
        by_receiver = mm(table, gpre[low:high, :]).astype(BF16)
        grads[part, :] = ncot[part, :].astype(F32) + mm_t(
            jnp.concatenate([gnpre[part, :], by_receiver, by_sender], axis=1),
            jnp.concatenate([nfirst[0:width, :], w_recv[...], w_send[...]], axis=1),
        )
    down.wait()
    up.wait()
    for copy in spread:
        copy.wait()


def kernel_finish(
    tail, out_node, out_edge, out_egrad, grads, rim_in, served, w_send, keys,
    new_nodes, new_edges, node_grads, edge_grads,
    out_ngrad, rows, store,
):
    count, width = grads.shape
    chunks = width // LANES
    puts = [
        pltpu.make_async_copy(source, target, store.at[i])
        for i, (source, target) in enumerate(
            ((out_edge, new_edges), (out_egrad, edge_grads), (out_node, new_nodes))
        )
    ]
    for put in puts:
        put.start()
    sums = served[0:TILE, :].astype(F32)
    for k in range(1, served.shape[0] // TILE):
        sums = sums + served[k * TILE : (k + 1) * TILE, :].astype(F32)
    rows[0:TILE, :] = sums[:, 0:width]
    rows[TILE:, :] = jnp.zeros((rows.shape[0] - TILE, width), F32)
    for c in range(chunks):
        rows[TILE : TILE + tail, c * LANES : (c + 1) * LANES] = sums[
            c * tail : (c + 1) * tail, width:
        ]
    arrived = jnp.concatenate([rim_in[...], rows[...].astype(BF16)], axis=0)
    changes = mm_t(arrived, w_send[...])
    coarse = changes[2 * HALO :, :].astype(BF16)
    wanted = keys[:, 0 : rows.shape[0]]
    for b in range(count // ROWS):
        part = pl.ds(b * ROWS, ROWS)
        added = grads[part, :] + mm(put_rows(wanted, b * ROWS, ROWS), coarse)
        low, high = b * ROWS, (b + 1) * ROWS
        pieces = []
        if low == 0:
            pieces.append((added[0:HALO, :] + changes[HALO : 2 * HALO, :]).astype(BF16))
        start = HALO if low == 0 else 0
        stop = ROWS - HALO if high == count else ROWS
        pieces.append(added[start:stop, :].astype(BF16))
        if high == count:
            pieces.append((added[stop:, :] + changes[0:HALO, :]).astype(BF16))
        out_ngrad[part, :] = jnp.concatenate(pieces, axis=0)
        put = pltpu.make_async_copy(out_ngrad.at[part], node_grads.at[part], store.at[len(puts)])
        put.start()
        puts.append(put)
    for put in puts:
        put.wait()


VM = pl.BlockSpec(memory_space=pltpu.VMEM)
ANY = pl.BlockSpec(memory_space=pl.ANY)


def dma(*shape):
    return pltpu.SemaphoreType.DMA(shape)


def shards(
    node_latents, edge_latents, fine_senders, coarse_owners, coarse_slots, coarse_nodes,
    receivers, block_fill, node_cotangent, edge_cotangent, edge_first, edge_bias, edge_second,
    edge_shift, edge_gain, node_first, node_bias, node_second, node_shift, node_gain,
):
    n = lax.axis_size("patch")
    chips = n // 2
    count, width = node_latents.shape
    edges = edge_latents.shape[0]
    fine = fine_senders.shape[1]
    tail = coarse_nodes.shape[1] - TILE
    owners = coarse_owners.reshape(1, -1)
    wide = width + LANES
    ints = jnp.int32

    def vec(value):
        return value.reshape(1, -1)

    def vm(rows, columns=width, kind=BF16):
        return pltpu.VMEM((rows, columns), kind)

    def like(value, memory=pltpu.VMEM):
        return memory(value.shape, value.dtype)

    *mids, = pl.pallas_call(
        functools.partial(kernel_layer, n, tail, edges // block_fill.shape[1]),
        out_shape=[
            vm(count), vm(edges), vm(edges), vm(count, width, F32), vm(2 * HALO),
            vm(chips * TILE, wide), vm(width), vm(1, LANES, ints),
        ],
        in_specs=[ANY] * 20,
        out_specs=[VM] * 8,
        scratch_shapes=[
            vm(count), like(coarse_nodes, pltpu.SMEM), vm(width), vm(width), vm(edges),
            vm(1, edges, ints), vm(1, fine, ints), vm(1, width, F32),
            vm(width), vm(1, width, F32), vm(1, width, F32), like(block_fill, pltpu.SMEM),
            like(owners), like(coarse_slots),
            vm(2 * width), vm(1, width, F32), vm(width), vm(1, width, F32), vm(1, width, F32),
            vm(count), vm(edges),
            vm(2 * HALO), vm(count), vm(count), vm(2 * HALO),
            vm(edges, width, F32), vm(edges, width, F32), vm(edges, LANES, F32), vm(edges),
            vm(count), vm(edges), vm(count), vm(edges), vm(edges, width, F32), vm(count, width, F32),
            vm(TILE, LANES, F32), vm(n * TILE, wide),
            vm(chips * TILE, wide), vm(chips * TILE, wide), vm(chips * TILE, wide),
            vm(chips * TILE, wide), vm(2 * HALO),
            dma(22), dma(2), dma(2), dma(chips), dma(chips), dma(chips), dma(chips),
            dma(2), dma(2), dma(chips), dma(chips), dma(1), dma(1),
        ],
        compiler_params=pltpu.CompilerParams(
            collective_id=0, has_side_effects=True, vmem_limit_bytes=LIMIT
        ),
        name="layer",
    )(
        node_latents, coarse_nodes, edge_first, edge_latents, receivers, fine_senders,
        vec(edge_bias), edge_second, vec(edge_shift), vec(edge_gain), block_fill, owners,
        coarse_slots, node_first, vec(node_bias), node_second, vec(node_shift),
        vec(node_gain), node_cotangent, edge_cotangent,
    )
    return pl.pallas_call(
        functools.partial(kernel_finish, tail),
        out_shape=[
            jax.ShapeDtypeStruct((count, width), BF16),
            jax.ShapeDtypeStruct((edges, width), BF16),
            jax.ShapeDtypeStruct((count, width), BF16),
            jax.ShapeDtypeStruct((edges, width), BF16),
        ],
        in_specs=[VM] * 8,
        out_specs=[ANY] * 4,
        scratch_shapes=[vm(count), vm(2 * TILE, width, F32), dma(3 + count // ROWS)],
        compiler_params=pltpu.CompilerParams(vmem_limit_bytes=LAST),
        name="finish",
    )(*mids)


def solution(mesh):
    rows = P(("groups", "patch"), None)
    flat = P("patch", None)
    return jax.shard_map(
        shards,
        mesh=mesh,
        in_specs=(rows, rows, flat, P("patch", None, None), flat, flat, flat, flat, rows, rows)
        + (P(),) * 10,
        out_specs=(rows, rows, rows, rows),
        check_vma=False,
    )
```

```python
import functools

import jax
import jax.numpy as jnp
from jax import lax
from jax.experimental import pallas as pl
from jax.experimental.pallas import tpu as pltpu
from jax.sharding import PartitionSpec as P

HALO = 64
SUB = 32
REACH = 4
ROWS = 256
TILE = 16
LANES = 128
MESH = pl.DeviceIdType.MESH
F32 = jnp.float32
BF16 = jnp.bfloat16
LIMIT = 59000 * 1024
LAST = 8 * 1024 * 1024


def mm(a, b):
    return jnp.dot(a, b, preferred_element_type=F32)


def mm_t(a, b):
    return lax.dot_general(a, b, (((1,), (1,)), ((), ())), preferred_element_type=F32)


def onehot(mask):
    return jnp.where(mask, 1.0, 0.0).astype(BF16)


def pick_rows(index_row, width, base=0):
    parts = []
    for k in range(index_row.shape[1] // LANES):
        chunk = jnp.broadcast_to(index_row[:, k * LANES : (k + 1) * LANES], (LANES, LANES))
        column = jnp.transpose(chunk)
        lane = lax.broadcasted_iota(jnp.int32, (LANES, LANES), 1)
        parts.append(
            jnp.concatenate(
                [onehot(column == lane + (base + j * LANES)) for j in range(width // LANES)], axis=1
            )
        )
    return jnp.concatenate(parts, axis=0)


def put_rows(index_row, low, count):
    rows = lax.broadcasted_iota(jnp.int32, (count, index_row.shape[1]), 0) + low
    return onehot(rows == index_row)


def sigmoid(values):
    return 0.5 * jnp.tanh(0.5 * values) + 0.5


def norm(values):
    centered = values - jnp.mean(values, axis=-1, keepdims=True)
    inverse = lax.rsqrt(jnp.mean(centered * centered, axis=-1, keepdims=True) + 1e-05)
    return centered * inverse, inverse


def norm_back(upstream, normed, inverse):
    return inverse * (
        upstream
        - jnp.mean(upstream, axis=-1, keepdims=True)
        - normed * jnp.mean(upstream * normed, axis=-1, keepdims=True)
    )


def edge_band(first, edges, count):
    last = first + ROWS - 1
    low = max(first // REACH, first - (edges - count))
    high = min(last, count - 1 - (edges - 1 - last) // REACH)
    return low // LANES * LANES, -(-(high + 1) // LANES) * LANES


def node_band(first, edges, count):
    last = first + ROWS - 1
    low = max(first, edges - REACH * (count - first))
    high = min(REACH * last + REACH - 1, last + edges - count)
    return low // LANES * LANES, -(-(high + 1) // LANES) * LANES


def greet(n):
    me = lax.axis_index("patch")
    barrier = pltpu.get_barrier_semaphore()
    chips = n // 2
    core = lax.rem(me, 2)
    chip = me // 2
    peers = [lax.rem(chip + k, chips) * 2 + core for k in range(1, chips)]
    peers += [chip * 2 + 1 - core, lax.rem(me + 1, n), lax.rem(me + n - 1, n)]
    for peer in peers:
        pl.semaphore_signal(barrier, inc=1, device_id={"patch": peer}, device_id_type=MESH)
    return barrier, len(peers)


def remote(src, dst, send, recv, peer):
    return pltpu.make_async_remote_copy(
        src_ref=src, dst_ref=dst, send_sem=send, recv_sem=recv,
        device_id={"patch": peer}, device_id_type=MESH,
    )


def rows_of(start, size):
    return pl.ds(pl.multiple_of(start, TILE), size)


def order_of(owner, n):
    return lax.rem(owner, 2) * (n // 2) + owner // 2


def bits_order(owner, n):
    return (owner & 1) * (n // 2) + (owner >> 1)


def kernel_layer(
    n, tail, block,
    node_hbm, cnodes_hbm, first_hbm, edge_hbm, receivers_hbm, senders_hbm, bias_hbm,
    second_hbm, shift_hbm, gain_hbm, fill_hbm, owners_hbm, slots_hbm,
    nfirst_hbm, nbias_hbm, nsecond_hbm, nshift_hbm, ngain_hbm, ncot_hbm, ecot_hbm,
    out_node, out_edge, out_egrad, grads, rim_in, served, w_send, keys,
    node, cnodes, w_edge, w_recv, edge, receivers, senders, bias,
    second, shift, gain, fill, owners, slots,
    nfirst, nbias, nsecond, nshift, ngain, ncot, ecot,
    halo, part_recv, part_send, part_halo,
    pre, normed, inverse, update, gagg, gpre, gnpre, bent_rows, upper, total,
    halo_picks, coarse_picks, gather_picks, node_puts, part_node, leave_puts, stay_puts, rim_puts,
    rows, tabs, leaving, staying, theirs, joined, rim,
    load, halo_send, halo_recv, chip_send, chip_recv, core_send, core_recv,
    rim_send, rim_recv, back_send, back_recv, swap_send, swap_recv,
):
    me = lax.axis_index("patch")
    chips = n // 2
    core = lax.rem(me, 2)
    chip = me // 2
    partner = chip * 2 + 1 - core
    edges, width = edge.shape
    count = node.shape[0]
    fine = senders.shape[1]
    chunks = width // LANES
    half = chips * TILE
    order = sorted(range(1, chips), key=lambda k: -min(k, chips - k))

    pairs = [
        (node_hbm, node), (cnodes_hbm, cnodes),
        (first_hbm.at[pl.ds(2 * width, width)], w_recv), (first_hbm.at[pl.ds(width, width)], w_send),
        (bias_hbm, bias), (receivers_hbm, receivers), (senders_hbm, senders),
        (first_hbm.at[pl.ds(0, width)], w_edge), (edge_hbm, edge),
        (second_hbm, second), (shift_hbm, shift), (gain_hbm, gain), (fill_hbm, fill),
        (owners_hbm, owners), (slots_hbm, slots),
        (nfirst_hbm, nfirst), (nbias_hbm, nbias), (nsecond_hbm, nsecond), (nshift_hbm, nshift),
        (ngain_hbm, ngain), (ncot_hbm, ncot), (ecot_hbm, ecot),
    ]
    loads = [
        pltpu.make_async_copy(source, target, load.at[i])
        for i, (source, target) in enumerate(pairs)
    ]
    waited = []

    def need(count_of):
        while len(waited) < count_of:
            loads[len(waited)].wait()
            waited.append(True)

    barrier, greeted = greet(n)
    for copy in loads[:9]:
        copy.start()

    need(1)
    up = remote(
        node.at[pl.ds(count - HALO, HALO)], halo.at[pl.ds(0, HALO)],
        halo_send.at[0], halo_recv.at[0], lax.rem(me + 1, n),
    )
    down = remote(
        node.at[pl.ds(0, HALO)], halo.at[pl.ds(HALO, HALO)],
        halo_send.at[1], halo_recv.at[1], lax.rem(me + n - 1, n),
    )
    need(2)
    line = lax.broadcasted_iota(jnp.int32, (2 * TILE, LANES), 0)
    wanted = jnp.full((2 * TILE, LANES), -1, jnp.int32)
    for k in range(TILE + tail):
        wanted = jnp.where(line == k, cnodes[0, k], wanted)
    lane = lax.broadcasted_iota(jnp.int32, (2 * TILE, LANES), 1)
    chosen = jnp.concatenate(
        [onehot(wanted == lane + k * LANES) for k in range(count // LANES)], axis=1
    )
    place_of = lax.broadcasted_iota(jnp.int32, (1, LANES), 1)
    listed = jnp.full((1, LANES), -1, jnp.int32)
    for k in range(TILE + tail):
        listed = jnp.where(place_of == k, cnodes[0, k], listed)
    keys[...] = listed
    own = order_of(me, n)
    mine = rows_of(own * TILE, TILE)
    table = mm(chosen, node[...])
    rows[...] = jnp.zeros_like(rows)
    for c in range(chunks):
        rows[c * tail : (c + 1) * tail, :] = table[TILE : TILE + tail, c * LANES : (c + 1) * LANES]
    tabs[mine, 0:width] = table[0:TILE, :].astype(BF16)
    tabs[mine, width : width + LANES] = rows[...].astype(BF16)

    pl.semaphore_wait(barrier, greeted)
    up.start()
    down.start()
    spread = []
    for k in order:
        copy = remote(
            tabs.at[mine], tabs.at[mine], chip_send.at[k], chip_recv.at[k],
            lax.rem(chip + k, chips) * 2 + core,
        )
        copy.start()
        spread.append(copy)
    across = [remote(tabs.at[mine], tabs.at[mine], core_send.at[0], core_recv.at[0], partner)]
    across[0].start()
    for copy in loads[9:]:
        copy.start()

    def advance(b):
        part = pl.ds(b * ROWS, ROWS)
        for q in range(b * ROWS, (b + 1) * ROWS, SUB):
            few = pl.ds(q, SUB)
            half_pre = 0.5 * pre[few, :]
            bent = jnp.tanh(half_pre)
            more = 1.0 + bent
            active = half_pre * more
            pre[few, :] = more + active * (1.0 - bent)
            bent_rows[few, :] = active.astype(BF16)
        normed[part, :] = mm(bent_rows[part, :], second[...])
        for q in range(b * ROWS, (b + 1) * ROWS, SUB):
            few = pl.ds(q, SUB)
            result = normed[few, :] + shift[...]
            centered = result - jnp.mean(result, axis=-1, keepdims=True)
            scale = lax.rsqrt(jnp.mean(centered * centered, axis=-1, keepdims=True) + 1e-05)
            row = lax.broadcasted_iota(jnp.int32, (SUB, 1), 0) + q % block
            scale = jnp.where(row < fill[0, q // block], scale, 0.0)
            unit = centered * scale
            normed[few, :] = unit
            inverse[few, :] = jnp.broadcast_to(0.5 * scale, (SUB, LANES))
            change = unit * gain[...]
            update[few, :] = change.astype(BF16)

    need(7)
    part_recv[...] = (mm(node[...], w_recv[...]) + bias[...]).astype(BF16)
    part_send[...] = mm(node[...], w_send[...]).astype(BF16)
    need(9)
    index = senders[...]
    inner = index - HALO
    outer = jnp.where(index < HALO, index, jnp.where(index >= HALO + count, index - count, -1))

    for b in [*range(fine // ROWS, edges // ROWS), *range(fine // ROWS)]:
        part = pl.ds(b * ROWS, ROWS)
        low, high = edge_band(b * ROWS, edges, count)
        left = [edge[part, :], pick_rows(receivers[:, b * ROWS : (b + 1) * ROWS], high - low, low)]
        right = [w_edge[...], part_recv[low:high, :]]
        if b < fine // ROWS:
            left.append(pick_rows(inner[:, b * ROWS : (b + 1) * ROWS], count))
            right.append(part_send[...])
        pre[part, :] = mm(jnp.concatenate(left, axis=1), jnp.concatenate(right, axis=0))
    need(15)
    place = bits_order(owners[...], n) * TILE
    slot = slots[...]
    coarse_keys = [jnp.where(slot < TILE, place + slot, -1)] + [
        jnp.where(slot >= TILE, place + (slot - TILE) + c * tail, -1) for c in range(chunks)
    ]
    every = n * TILE
    for c, key in enumerate(coarse_keys):
        coarse_picks[:, c * every : (c + 1) * every] = pick_rows(key, every)
        leave_puts[c * half : (c + 1) * half, :] = put_rows(key, (1 - core) * half, half)
        stay_puts[c * half : (c + 1) * half, :] = put_rows(key, core * half, half)
    rim_puts[...] = put_rows(outer, 0, 2 * HALO)
    for b in range(fine // ROWS):
        part = pl.ds(b * ROWS, ROWS)
        halo_picks[part, :] = pick_rows(outer[:, b * ROWS : (b + 1) * ROWS], 2 * HALO)
    for b in range(edges // ROWS):
        part = pl.ds(b * ROWS, ROWS)
        low, high = edge_band(b * ROWS, edges, count)
        gather_picks[part, low:high] = pick_rows(
            receivers[:, b * ROWS : (b + 1) * ROWS], high - low, low
        )
    need(17)
    for b in range(count // ROWS):
        part = pl.ds(b * ROWS, ROWS)
        low, high = node_band(b * ROWS, edges, count)
        node_puts[part, low:high] = put_rows(receivers[:, low:high], b * ROWS, ROWS)
        part_node[part, :] = mm(node[part, :], nfirst[0:width, :]) + nbias[...]
    up.wait()
    down.wait()
    part_halo[...] = mm(halo[...], w_send[...]).astype(BF16)

    def close_up(b):
        part = pl.ds(b * ROWS, ROWS)
        pre[part, :] += mm(halo_picks[part, :], part_halo[...])
        advance(b)

    close_up(0)
    for k in order:
        source = core * chips + lax.rem(chip + chips - k, chips)
        there = tabs.at[rows_of(source * TILE, TILE)]
        remote(there, there, chip_send.at[k], chip_recv.at[k], partner).wait_recv()
        copy = remote(there, there, core_send.at[k], core_recv.at[k], partner)
        copy.start()
        across.append(copy)
    for b in range(1, fine // ROWS):
        close_up(b)

    def turn(b):
        part = pl.ds(b * ROWS, ROWS)
        low, high = node_band(b * ROWS, edges, count)
        summed = mm(node_puts[part, low:high], update[low:high, :])
        total[part, :] = part_node[part, :] + mm(summed.astype(BF16), nfirst[width:, :])
        for q in range(b * ROWS, (b + 1) * ROWS, SUB):
            few = pl.ds(q, SUB)
            half_values = 0.5 * total[few, :]
            bent = jnp.tanh(half_values)
            more = 1.0 + bent
            active = half_values * more
            total[few, :] = more + active * (1.0 - bent)
            gnpre[few, :] = active.astype(BF16)
        grads[part, :] = mm(gnpre[part, :], nsecond[...])
        for q in range(b * ROWS, (b + 1) * ROWS, SUB):
            few = pl.ds(q, SUB)
            result, scale = norm(grads[few, :] + nshift[...])
            part_node[few, :] = result
            back = norm_back(ncot[few, :].astype(F32) * ngain[...], result, 0.5 * scale)
            gagg[few, :] = back.astype(BF16)
        inner_grad = (mm_t(gagg[part, :], nsecond[...]) * total[part, :]).astype(BF16)
        gnpre[part, :] = inner_grad
        gagg[part, :] = mm_t(inner_grad, nfirst[width:, :]).astype(BF16)

    def retreat(b):
        part = pl.ds(b * ROWS, ROWS)
        low, high = edge_band(b * ROWS, edges, count)
        upper[part, :] = mm(gather_picks[part, low:high], gagg[low:high, :])
        for q in range(b * ROWS, (b + 1) * ROWS, SUB):
            few = pl.ds(q, SUB)
            upstream = (ecot[few, :].astype(F32) + upper[few, :]) * gain[...]
            back = norm_back(upstream, normed[few, :], inverse[few, 0:1])
            bent_rows[few, :] = back.astype(BF16)
        gpre[part, :] = (mm_t(bent_rows[part, :], second[...]) * pre[part, :]).astype(BF16)

    need(22)
    for copy in across:
        copy.wait()
    for copy in spread:
        copy.wait_send()
    gathered = mm(coarse_picks[:, 0:every], tabs[:, 0:width])
    tails = [
        mm(coarse_picks[:, c * every : (c + 1) * every], tabs[:, width : width + LANES])
        for c in range(1, chunks + 1)
    ]
    sent = (gathered + jnp.concatenate(tails, axis=1)).astype(BF16)
    coarse = pl.ds(fine, edges - fine)
    pre[coarse, :] += mm(sent, w_send[...])
    for b in range(fine // ROWS, edges // ROWS):
        advance(b)
    for b in range(count // ROWS):
        turn(b)
    for b in range(fine // ROWS, edges // ROWS):
        retreat(b)

    def returned(puts, target):
        target[:, 0:width] = mm(puts[0:half, :], gpre[coarse, :]).astype(BF16)
        packed = jnp.zeros((half, LANES), F32)
        for c in range(chunks):
            packed = packed + mm(
                puts[(c + 1) * half : (c + 2) * half, :], gpre[coarse, c * LANES : (c + 1) * LANES]
            )
        target[:, width:] = packed.astype(BF16)

    returned(leave_puts, leaving)
    swap = remote(leaving, theirs, swap_send.at[0], swap_recv.at[0], partner)
    swap.start()
    returned(stay_puts, staying)
    for b in range(fine // ROWS):
        retreat(b)
    rim[...] = mm(rim_puts[...], gpre[0:fine, :]).astype(BF16)
    down = remote(
        rim.at[pl.ds(0, HALO)], rim_in.at[pl.ds(0, HALO)],
        rim_send.at[0], rim_recv.at[0], lax.rem(me + n - 1, n),
    )
    up = remote(
        rim.at[pl.ds(HALO, HALO)], rim_in.at[pl.ds(HALO, HALO)],
        rim_send.at[1], rim_recv.at[1], lax.rem(me + 1, n),
    )
    up.start()
    down.start()
    swap.wait()
    joined[...] = (staying[...].astype(F32) + theirs[...].astype(F32)).astype(BF16)
    served[0:TILE, :] = joined[rows_of(chip * TILE, TILE), :]
    spread = []

    def hand(t):
        target = t + jnp.where(chip <= t, 1, 0)
        k = lax.rem(target - chip + chips, chips)
        copy = remote(
            joined.at[rows_of(target * TILE, TILE)], served.at[rows_of(k * TILE, TILE)],
            back_send.at[k], back_recv.at[k], target * 2 + core,
        )
        copy.start()
        spread.append(copy)

    for t in range(chips - 1):
        hand(t)

    for b in range(edges // ROWS):
        part = pl.ds(b * ROWS, ROWS)
        out_egrad[part, :] = (
            ecot[part, :].astype(F32) + mm_t(gpre[part, :], w_edge[...])
        ).astype(BF16)
    for b in range(count // ROWS):
        part = pl.ds(b * ROWS, ROWS)
        by_sender = mm(put_rows(inner, b * ROWS, ROWS), gpre[0:fine, :]).astype(BF16)
        low, high = node_band(b * ROWS, edges, count)
        by_receiver = mm(node_puts[part, low:high], gpre[low:high, :]).astype(BF16)
        grads[part, :] = ncot[part, :].astype(F32) + mm_t(
            jnp.concatenate([gnpre[part, :], by_receiver, by_sender], axis=1),
            jnp.concatenate([nfirst[0:width, :], w_recv[...], w_send[...]], axis=1),
        )
    for b in range(count // ROWS):
        part = pl.ds(b * ROWS, ROWS)
        out_node[part, :] = (node[part, :].astype(F32) + part_node[part, :] * ngain[...]).astype(BF16)
    for b in range(edges // ROWS):
        part = pl.ds(b * ROWS, ROWS)
        out_edge[part, :] = (edge[part, :].astype(F32) + normed[part, :] * gain[...]).astype(BF16)
    down.wait()
    up.wait()
    for copy in spread:
        copy.wait()


def kernel_finish(
    tail, out_node, out_edge, out_egrad, grads, rim_in, served, w_send, keys,
    new_nodes, new_edges, node_grads, edge_grads,
    out_ngrad, rows, store,
):
    count, width = grads.shape
    chunks = width // LANES
    puts = [
        pltpu.make_async_copy(source, target, store.at[i])
        for i, (source, target) in enumerate(
            ((out_edge, new_edges), (out_egrad, edge_grads), (out_node, new_nodes))
        )
    ]
    for put in puts:
        put.start()
    sums = served[0:TILE, :].astype(F32)
    for k in range(1, served.shape[0] // TILE):
        sums = sums + served[k * TILE : (k + 1) * TILE, :].astype(F32)
    rows[0:TILE, :] = sums[:, 0:width]
    rows[TILE:, :] = jnp.zeros((rows.shape[0] - TILE, width), F32)
    for c in range(chunks):
        rows[TILE : TILE + tail, c * LANES : (c + 1) * LANES] = sums[
            c * tail : (c + 1) * tail, width:
        ]
    arrived = jnp.concatenate([rim_in[...], rows[...].astype(BF16)], axis=0)
    changes = mm_t(arrived, w_send[...])
    coarse = changes[2 * HALO :, :].astype(BF16)
    wanted = keys[:, 0 : rows.shape[0]]
    for b in range(count // ROWS):
        part = pl.ds(b * ROWS, ROWS)
        added = grads[part, :] + mm(put_rows(wanted, b * ROWS, ROWS), coarse)
        low, high = b * ROWS, (b + 1) * ROWS
        pieces = []
        if low == 0:
            pieces.append((added[0:HALO, :] + changes[HALO : 2 * HALO, :]).astype(BF16))
        start = HALO if low == 0 else 0
        stop = ROWS - HALO if high == count else ROWS
        pieces.append(added[start:stop, :].astype(BF16))
        if high == count:
            pieces.append((added[stop:, :] + changes[0:HALO, :]).astype(BF16))
        out_ngrad[part, :] = jnp.concatenate(pieces, axis=0)
        put = pltpu.make_async_copy(out_ngrad.at[part], node_grads.at[part], store.at[len(puts)])
        put.start()
        puts.append(put)
    for put in puts:
        put.wait()


VM = pl.BlockSpec(memory_space=pltpu.VMEM)
ANY = pl.BlockSpec(memory_space=pl.ANY)


def dma(*shape):
    return pltpu.SemaphoreType.DMA(shape)


def shards(
    node_latents, edge_latents, fine_senders, coarse_owners, coarse_slots, coarse_nodes,
    receivers, block_fill, node_cotangent, edge_cotangent, edge_first, edge_bias, edge_second,
    edge_shift, edge_gain, node_first, node_bias, node_second, node_shift, node_gain,
):
    n = lax.axis_size("patch")
    chips = n // 2
    count, width = node_latents.shape
    edges = edge_latents.shape[0]
    fine = fine_senders.shape[1]
    tail = coarse_nodes.shape[1] - TILE
    owners = coarse_owners.reshape(1, -1)
    wide = width + LANES
    ints = jnp.int32

    def vec(value):
        return value.reshape(1, -1)

    def vm(rows, columns=width, kind=BF16):
        return pltpu.VMEM((rows, columns), kind)

    def like(value, memory=pltpu.VMEM):
        return memory(value.shape, value.dtype)

    *mids, = pl.pallas_call(
        functools.partial(kernel_layer, n, tail, edges // block_fill.shape[1]),
        out_shape=[
            vm(count), vm(edges), vm(edges), vm(count, width, F32), vm(2 * HALO),
            vm(chips * TILE, wide), vm(width), vm(1, LANES, ints),
        ],
        in_specs=[ANY] * 20,
        out_specs=[VM] * 8,
        scratch_shapes=[
            vm(count), like(coarse_nodes, pltpu.SMEM), vm(width), vm(width), vm(edges),
            vm(1, edges, ints), vm(1, fine, ints), vm(1, width, F32),
            vm(width), vm(1, width, F32), vm(1, width, F32), like(block_fill, pltpu.SMEM),
            like(owners), like(coarse_slots),
            vm(2 * width), vm(1, width, F32), vm(width), vm(1, width, F32), vm(1, width, F32),
            vm(count), vm(edges),
            vm(2 * HALO), vm(count), vm(count), vm(2 * HALO),
            vm(edges, width, F32), vm(edges, width, F32), vm(edges, LANES, F32), vm(edges),
            vm(count), vm(edges), vm(count), vm(edges), vm(edges, width, F32), vm(count, width, F32),
            vm(fine, 2 * HALO), vm(edges - fine, n * TILE * (1 + width // LANES)),
            vm(edges, count), vm(count, edges), vm(count, width, F32),
            vm(chips * TILE * (1 + width // LANES), edges - fine),
            vm(chips * TILE * (1 + width // LANES), edges - fine), vm(2 * HALO, fine),
            vm(TILE, LANES, F32), vm(n * TILE, wide),
            vm(chips * TILE, wide), vm(chips * TILE, wide), vm(chips * TILE, wide),
            vm(chips * TILE, wide), vm(2 * HALO),
            dma(22), dma(2), dma(2), dma(chips), dma(chips), dma(chips), dma(chips),
            dma(2), dma(2), dma(chips), dma(chips), dma(1), dma(1),
        ],
        compiler_params=pltpu.CompilerParams(
            collective_id=0, has_side_effects=True, vmem_limit_bytes=LIMIT
        ),
        name="layer",
    )(
        node_latents, coarse_nodes, edge_first, edge_latents, receivers, fine_senders,
        vec(edge_bias), edge_second, vec(edge_shift), vec(edge_gain), block_fill, owners,
        coarse_slots, node_first, vec(node_bias), node_second, vec(node_shift),
        vec(node_gain), node_cotangent, edge_cotangent,
    )
    return pl.pallas_call(
        functools.partial(kernel_finish, tail),
        out_shape=[
            jax.ShapeDtypeStruct((count, width), BF16),
            jax.ShapeDtypeStruct((edges, width), BF16),
            jax.ShapeDtypeStruct((count, width), BF16),
            jax.ShapeDtypeStruct((edges, width), BF16),
        ],
        in_specs=[VM] * 8,
        out_specs=[ANY] * 4,
        scratch_shapes=[vm(count), vm(2 * TILE, width, F32), dma(3 + count // ROWS)],
        compiler_params=pltpu.CompilerParams(vmem_limit_bytes=LAST),
        name="finish",
    )(*mids)


def solution(mesh):
    rows = P(("groups", "patch"), None)
    flat = P("patch", None)
    return jax.shard_map(
        shards,
        mesh=mesh,
        in_specs=(rows, rows, flat, P("patch", None, None), flat, flat, flat, flat, rows, rows)
        + (P(),) * 10,
        out_specs=(rows, rows, rows, rows),
        check_vma=False,
    )
```
